32 devices in a mesh: group: 4 (over y, x), slot: 8 (over z, core).
Axes of the slice: x: 2, y: 2, z: 4, core: 2. Of those that a mesh axis runs over, the one named last changes fastest.
Arguments:
- tokens: bfloat16 [4096, 2048], P(('group', 'slot')), may hold values from -6 to 6
- cotangent: bfloat16 [4096, 512], P(('group', 'slot')), may hold values from -0.59765625 to 0.59765625
- weight_halves: bfloat16 [32, 1024, 512], P(('group', 'slot')), may hold values from -0.125 to 0.125
- momentum_halves: bfloat16 [32, 1024, 512], P(('group', 'slot')), may hold values from -6 to 6
- old_map: int32 [4, 4], replicated, may hold values from 0 to 3, each once within a row
- new_map: int32 [4, 8], replicated, may hold values from 0 to 3, as said below
- row_ids: int32 [32, 128], P(('group', 'slot')), may hold values from 0 to 127
Outputs:
- projected: bfloat16 [4096, 512], P(('group', 'slot'))
The draws below stay inside these ranges and needn't reach their ends.
Inputs may be any that keep to these rules, and one draw needn't show every extreme that they name: `old_map`: each row names each of the group's experts once. `new_map`: every expert is hosted by one to four new slots; among the experts of every owner group one is hosted by exactly four.
All inputs are finite; a program needn't handle non-finite values.
Results may differ from the reference program's by a relative error of at most 0.007.
Values may be sent and summed in bfloat16 or wider, within the bound.
No kernel may reach another device: no remote copies, remote signals or barrier semaphores. Data moves between devices by JAX's collectives and lax.ppermute only.
A program may use at most 64 MiB of HBM per device.

```python
import math
import jax
import jax.numpy as jnp
from jax import lax

D = 2048
H = 512
R_OLD = 128
R_NEW = 128
ITERS = 2
EXP_GRP = 4
HOSTS = 2
BLK = 128
N_GROUP = 4
N_SLOT = 8


def draw_new_map(key, part):
    per_group = N_SLOT // 2
    pair_count = (per_group - 4) // 2

    def one_source(sub_key):
        first_key, second_key, third_key = jax.random.split(sub_key, 3)
        order = jax.random.permutation(first_key, per_group).astype(jnp.int32)
        lower = jax.random.randint(second_key, (pair_count,), 1, 4).astype(jnp.int32)
        counts = jnp.concatenate([jnp.array([4, 1, 2, 1], jnp.int32), jnp.stack([lower, 4 - lower], axis=1).reshape(-1)])
        listed = jnp.repeat(order, counts, total_repeat_length=N_SLOT)
        return jax.random.permutation(third_key, listed)
    lists = jax.vmap(one_source)(jax.random.split(jax.random.fold_in(key, 7), N_GROUP))
    arranged = jnp.transpose(lists.reshape(N_GROUP, N_GROUP, N_SLOT // N_GROUP), (1, 0, 2))
    return arranged.reshape(N_GROUP, N_SLOT).astype(jnp.int32)


def with_ends(values, rng, least, high):
    longest = values.shape.index(max(values.shape))
    spots = []
    for shift in (0, 1):
        where = [jax.random.randint(jax.random.fold_in(rng, axis), (), 0, length) for axis, length in enumerate(values.shape)]
        where[longest] = (where[longest] + shift) % values.shape[longest]
        spots.append(tuple(where))
    return values.at[spots[0]].set(least).at[spots[1]].set(high)


def levels(key, shape, pieces, least, top_value):
    def one(position, parts):
        draws = jax.random.uniform(jax.random.fold_in(jax.random.fold_in(key, 6), position), (parts,), jnp.float32, least / len(pieces), top_value / len(pieces))
        return jnp.repeat(jnp.exp(draws), shape[position] // parts).reshape((-1,) + (1,) * (len(shape) - position - 1))

    loudness = one(*pieces[0])
    for cut in pieces[1:]:
        loudness = loudness * one(*cut)
    return loudness


def scatter_about(key, extent, width, most, shards=(), kind=jnp.bfloat16):
    entries = width * jax.random.normal(key, extent, jnp.float32)
    if shards:
        entries = entries * levels(key, extent, shards, -0.22, 0.18)
    return jnp.clip(entries, -most, most).astype(kind)


def setup_inputs(seed: int = 0) -> dict:
    streams_of = jax.random.split(jax.random.key(seed), 8)
    tokens = scatter_about(streams_of[0], (N_GROUP * N_SLOT * R_OLD, D), 1.0, 6.0, ((0, 32),))
    cotangent = scatter_about(streams_of[1], (N_GROUP * N_SLOT * R_OLD, H), 0.1, 0.59765625, ((0, 32),))
    weight_halves = scatter_about(streams_of[2], (N_GROUP * N_SLOT, D // 2, H), D ** -0.5, 0.125, ((0, 32),))
    momentum_halves = scatter_about(streams_of[3], (N_GROUP * N_SLOT, D // 2, H), 1.0, 6.0, ((0, 32),))
    old_map = jax.vmap(lambda own: jax.random.permutation(own, EXP_GRP))(jax.random.split(streams_of[4], N_GROUP)).reshape((N_GROUP, EXP_GRP)).astype(jnp.int32)
    new_map = draw_new_map(jax.random.fold_in(streams_of[7], 71), 0)
    row_ids = with_ends(jax.random.randint(streams_of[6], (N_GROUP * N_SLOT, R_NEW), 0, R_OLD), jax.random.fold_in(streams_of[6], 1), 0, R_OLD - 1).astype(jnp.int32)
    return {"tokens": tokens, "cotangent": cotangent, "weight_halves": weight_halves, "momentum_halves": momentum_halves, "old_map": old_map, "new_map": new_map, "row_ids": row_ids}


coef_a = 3.4445
coef_b = -4.775
coef_c = 2.0315
momentum_rate = 0.95
step_scale = 0.01
gram_eps = 1e-06

def split_rows(full_matrix, which_half):
    blocks_view = full_matrix.reshape(N_SLOT, 2, BLK, H)
    return blocks_view[:, which_half].reshape(D // 2, H)

def join_rows(first_half, second_half):
    stacked = jnp.stack([first_half.reshape(N_SLOT, BLK, H), second_half.reshape(N_SLOT, BLK, H)], axis=1)
    return stacked.reshape(D, H)

def rounded(value):
    return lax.optimization_barrier(value.astype(jnp.bfloat16)).astype(jnp.float32)

def half_gram(half_rows):
    return rounded(jnp.dot(half_rows.T, half_rows, preferred_element_type=jnp.float32))

def full_gram(current):
    return half_gram(split_rows(current, 0)) + half_gram(split_rows(current, 1))

def update_expert(bundle):
    token_pair, cot_pair, weight_pair, moment_pair = bundle
    gradient = rounded(jnp.dot(token_pair[0].T, cot_pair[0], preferred_element_type=jnp.float32))
    gradient = gradient + rounded(jnp.dot(token_pair[1].T, cot_pair[1], preferred_element_type=jnp.float32))
    moment = join_rows(moment_pair[0], moment_pair[1]).astype(jnp.float32)
    current = (momentum_rate * moment + gradient).astype(jnp.bfloat16)
    gram_sum = full_gram(current)
    norm_sq = jnp.trace(gram_sum) + gram_eps
    for iteration in range(ITERS):
        if iteration == 0:
            scaled = gram_sum / norm_sq
            factor = 1.0 / jnp.sqrt(norm_sq)
        else:
            scaled = gram_sum
            factor = 1.0
        gram_bf = scaled.astype(jnp.bfloat16)
        square = jnp.dot(gram_bf, gram_bf, preferred_element_type=jnp.float32)
        polynomial = (coef_b * scaled + coef_c * square).astype(jnp.bfloat16)
        product = jnp.dot(current, polynomial, preferred_element_type=jnp.float32)
        current = (factor * (coef_a * current.astype(jnp.float32) + product)).astype(jnp.bfloat16)
        if iteration + 1 < ITERS:
            gram_sum = full_gram(current)
    weight = join_rows(weight_pair[0], weight_pair[1]).astype(jnp.float32)
    return (weight - step_scale * math.sqrt(D) * current.astype(jnp.float32)).astype(jnp.bfloat16)

def per_group(bundle):
    return lax.map(update_expert, bundle)

def reference(tokens, cotangent, weight_halves, momentum_halves, old_map, new_map, row_ids):
    token_rows = tokens.reshape(N_GROUP, EXP_GRP, 2, R_OLD, D)
    cot_rows = cotangent.reshape(N_GROUP, EXP_GRP, 2, R_OLD, H)
    weight_rows = weight_halves.reshape(N_GROUP, EXP_GRP, 2, D // 2, H)
    moment_rows = momentum_halves.reshape(N_GROUP, EXP_GRP, 2, D // 2, H)
    updated = lax.map(per_group, (token_rows, cot_rows, weight_rows, moment_rows))
    expert_iota = jnp.arange(EXP_GRP, dtype=jnp.int32)
    where_held = jnp.argmax((old_map[:, None, :] == expert_iota[None, :, None]).astype(jnp.int32), axis=2).astype(jnp.int32)
    slot_iota = jnp.arange(N_SLOT, dtype=jnp.int32)
    source = jnp.broadcast_to((slot_iota // HOSTS)[None, :], (N_GROUP, N_SLOT)).astype(jnp.int32)
    holder = where_held[source, new_map].astype(jnp.int32)
    flat_tokens = tokens.reshape(N_GROUP * N_SLOT, R_OLD, D)

    def project(bundle):
        own_tokens, own_ids, own_source, own_holder = bundle
        weight = updated[own_source, own_holder]
        chosen = jnp.take(own_tokens, own_ids, axis=0)
        return jnp.dot(chosen, weight, preferred_element_type=jnp.float32).astype(jnp.bfloat16)
    projected = lax.map(project, (flat_tokens, row_ids, source.reshape(-1), holder.reshape(-1)))
    return projected.reshape(N_GROUP * N_SLOT * R_NEW, H)
```

```python
import math

import jax
import jax.numpy as jnp
from jax import lax
from jax.sharding import PartitionSpec as P


coef_a = 3.4445
coef_b = -4.775
coef_c = 2.0315
momentum_rate = 0.95
step_scale = 0.01
gram_eps = 1e-06
contract_rows = (((0,), (0,)), ((), ()))
STAGES = 2
MOST_PERMUTES = 4


def swapped(shard):
    return lax.ppermute(shard, "slot", [(i, i ^ 1) for i in range(lax.axis_size("slot"))])


def exchange(piece, axis, stride):
    size = lax.axis_size(axis)
    count = size // stride
    place = lax.axis_index(axis) // stride
    if count <= MOST_PERMUTES:
        received = [piece(place)]
        for k in range(1, count):
            pairs = [(i, i ^ (k * stride)) for i in range(size)]
            received.append(lax.ppermute(piece(place ^ k), axis, pairs))
        return received
    stacked = jnp.stack([piece(d) for d in range(count)])
    groups = [[first + stride * d for d in range(count)] for first in range(stride)]
    landed = lax.all_to_all(
        stacked,
        axis,
        split_axis=0,
        concat_axis=0,
        tiled=True,
        axis_index_groups=groups if stride > 1 else None,
    )
    return [lax.dynamic_index_in_dim(landed, place ^ k, 0, keepdims=False) for k in range(count)]


def pick_columns(token_block, which_half, slot_count):
    row_count, col_count = token_block.shape
    pieces_view = token_block.reshape(row_count, slot_count, 2, col_count // (2 * slot_count))
    chosen = lax.dynamic_index_in_dim(pieces_view, which_half, axis=2, keepdims=False)
    return chosen.reshape(row_count, col_count // 2)


def matmul(left, right):
    return jnp.dot(
        left.astype(jnp.bfloat16), right.astype(jnp.bfloat16), preferred_element_type=jnp.float32
    )


def tdot(left, right):
    return lax.dot_general(left, right, contract_rows, preferred_element_type=jnp.float32)


def update_matrix(gram):
    norm_sq = jnp.trace(gram) + gram_eps
    first = gram / norm_sq
    poly_first = coef_b * first + coef_c * matmul(first, first)
    half_way = coef_a * first + matmul(first, poly_first)
    second = coef_a * half_way + matmul(poly_first, half_way)
    poly_second = coef_b * second + coef_c * matmul(second, second)
    remainder = coef_a * (poly_first + poly_second) + matmul(poly_first, poly_second)
    return lax.rsqrt(norm_sq), remainder.astype(jnp.bfloat16)


def on_device(tokens, cotangent, weight_halves, momentum_halves, old_map, new_map, row_ids):
    slot_count = lax.axis_size("slot")
    group_count = lax.axis_size("group")
    planes = slot_count // 2
    hosts = slot_count // group_count
    owners = max(1, 2 // hosts)
    row_count, model_width = tokens.shape
    hidden = cotangent.shape[1]
    half_rows = model_width // 2
    chunk = half_rows // group_count
    slot = lax.axis_index("slot")
    half = slot % 2
    plane = slot // 2
    group = lax.axis_index("group")

    own_tokens = pick_columns(tokens, half, slot_count)
    incoming = swapped(
        jnp.concatenate([pick_columns(tokens, 1 - half, slot_count), cotangent], axis=1)
    )
    peer_tokens = incoming[:, :half_rows]
    gradient = tdot(own_tokens, cotangent) + tdot(peer_tokens, incoming[:, half_rows:])
    x0 = (momentum_rate * momentum_halves[0].astype(jnp.float32) + gradient).astype(jnp.bfloat16)
    own_gram = tdot(x0, x0).astype(jnp.bfloat16)

    both = jnp.stack([own_tokens, peer_tokens]).reshape(2, row_count, group_count, chunk)
    token_parts = exchange(
        lambda d: lax.dynamic_index_in_dim(both, d, 2, keepdims=False), "group", 1
    )
    requested = jnp.stack(token_parts)

    from_group = group ^ jnp.arange(group_count)
    core = half ^ jnp.arange(2)
    wanted_slot = 2 * plane + core
    experts = new_map[from_group[:, None], wanted_slot[None, :]]
    lists = old_map[wanted_slot // hosts]
    holder = jnp.argmax((lists[None] == experts[:, :, None]).astype(jnp.int32), axis=2)

    peer_gram = swapped(own_gram)
    factor, remainder = update_matrix(
        own_gram.astype(jnp.float32) + peer_gram.astype(jnp.float32)
    )
    scale = step_scale * math.sqrt(model_width) * factor

    masked = [
        jnp.where((holder == (plane ^ k))[:, :, None, None], requested, 0) for k in range(planes)
    ]

    width = hidden // STAGES
    outputs = []
    for stage in range(STAGES):
        cols = slice(stage * width, (stage + 1) * width)
        moved = coef_a * coef_a * x0[:, cols].astype(jnp.float32) + matmul(x0, remainder[:, cols])
        renewed = (weight_halves[0][:, cols].astype(jnp.float32) - scale * moved).astype(
            jnp.bfloat16
        )
        chunks = renewed.reshape(group_count, chunk, width)
        in_plane = jnp.stack(
            exchange(lambda d: lax.dynamic_index_in_dim(chunks, d, 0, keepdims=False), "group", 1)
        )

        def owned_by(d):
            return jnp.stack(
                [
                    lax.dynamic_index_in_dim(in_plane, group ^ (d * owners + j), 0, keepdims=False)
                    for j in range(owners)
                ]
            )

        arrived = exchange(owned_by, "slot", 2)
        if owners == 1:
            partial = sum(
                jnp.einsum(
                    "krtc,cw->krtw", masked[k], arrived[k][0], preferred_element_type=jnp.float32
                )
                for k in range(planes)
            )
        else:
            stacked = jnp.stack(arrived)
            partial = jnp.stack(
                [
                    jnp.einsum(
                        "pktc,pcw->ktw",
                        jnp.stack([m[:, rel] for m in masked]),
                        jnp.take(stacked, half ^ rel, axis=1),
                        preferred_element_type=jnp.float32,
                    )
                    for rel in range(2)
                ],
                axis=1,
            )
        other = swapped(partial[:, 1].astype(jnp.bfloat16))
        summed = (partial[:, 0] + other.astype(jnp.float32)).astype(jnp.bfloat16)
        returned = exchange(
            lambda d: lax.dynamic_index_in_dim(summed, group ^ d, 0, keepdims=False), "group", 1
        )
        outputs.append(sum(r.astype(jnp.float32) for r in returned).astype(jnp.bfloat16))
    whole = jnp.concatenate(outputs, axis=1)
    pick = (row_ids[0][:, None] == jnp.arange(row_count)[None, :]).astype(jnp.bfloat16)
    return jnp.dot(pick, whole, preferred_element_type=jnp.float32).astype(jnp.bfloat16)


def solution(mesh):
    placed = (
        P(("group", "slot"), None),
        P(("group", "slot"), None),
        P(("group", "slot"), None, None),
        P(("group", "slot"), None, None),
        P(),
        P(),
        P(("group", "slot"), None),
    )
    return jax.shard_map(
        on_device, mesh=mesh, in_specs=placed, out_specs=P(("group", "slot"), None), check_vma=False
    )
```

```python
import functools
import math

import jax
import jax.numpy as jnp
from jax import lax
from jax.experimental import pallas as pl
from jax.experimental.pallas import tpu as pltpu
from jax.sharding import PartitionSpec as P


coef_a = 3.4445
coef_b = -4.775
coef_c = 2.0315
momentum_rate = 0.95
step_scale = 0.01
gram_eps = 1e-06
contract_rows = (((0,), (0,)), ((), ()))
STAGES = 2
MOST_PERMUTES = 4
LANES = 128
bf16 = jnp.bfloat16
f32 = jnp.float32


def shifted(shard, axis, stride, k):
    size = lax.axis_size(axis)
    return lax.ppermute(shard, axis, [(i, i ^ (k * stride)) for i in range(size)])


def swapped(shard):
    return shifted(shard, "slot", 1, 1)


def exchange(piece, axis, stride):
    size = lax.axis_size(axis)
    count = size // stride
    place = lax.axis_index(axis) // stride
    stacked = jnp.stack([piece(d) for d in range(count)])
    groups = [[first + stride * d for d in range(count)] for first in range(stride)]
    landed = lax.all_to_all(
        stacked,
        axis,
        split_axis=0,
        concat_axis=0,
        tiled=True,
        axis_index_groups=groups if stride > 1 else None,
    )
    return [lax.dynamic_index_in_dim(landed, place ^ k, 0, keepdims=False) for k in range(count)]


def pick_columns(token_block, which_half, slot_count):
    row_count, col_count = token_block.shape
    pieces_view = token_block.reshape(row_count, slot_count, 2, col_count // (2 * slot_count))
    chosen = lax.dynamic_index_in_dim(pieces_view, which_half, axis=2, keepdims=False)
    return chosen.reshape(row_count, col_count // 2)


def matmul(left, right):
    return jnp.dot(left.astype(bf16), right.astype(bf16), preferred_element_type=f32)


def tdot(left, right):
    return lax.dot_general(left, right, contract_rows, preferred_element_type=f32)


def update_matrix(gram):
    on_diagonal = lax.broadcasted_iota(jnp.int32, gram.shape, 0) == lax.broadcasted_iota(
        jnp.int32, gram.shape, 1
    )
    norm_sq = jnp.sum(jnp.where(on_diagonal, gram, 0.0), keepdims=True) + gram_eps
    first = gram * (1.0 / norm_sq)
    poly_first = coef_b * first + coef_c * matmul(first, first)
    half_way = coef_a * first + matmul(first, poly_first)
    second = coef_a * half_way + matmul(poly_first, half_way)
    poly_second = coef_b * second + coef_c * matmul(second, second)
    remainder = coef_a * (poly_first + poly_second) + matmul(poly_first, poly_second)
    return lax.rsqrt(norm_sq), remainder.astype(bf16)


def renew(weight, x0, x0_cols, factor, remainder, model_width):
    moved = coef_a * coef_a * x0_cols.astype(f32) + matmul(x0, remainder)
    scale = step_scale * math.sqrt(model_width) * factor
    return (weight.astype(f32) - scale * moved).astype(bf16)


def front_kernel(half_ref, own_ref, peer_ref, cot_ref, peer_cot_ref, momentum_ref, x0_ref, gram_ref):
    rows = x0_ref.shape[0]
    piece = own_ref.shape[1] // (2 * (rows // LANES))
    cots = jnp.concatenate([cot_ref[...], peer_cot_ref[...]], axis=0)
    half = half_ref[0]
    gram = None
    block = 2 * piece
    for i in range(rows // block):
        columns = [
            pl.ds(pl.multiple_of((2 * (2 * i + j) + half) * piece, piece), piece) for j in range(2)
        ]
        toks = jnp.concatenate(
            [
                jnp.concatenate([ref[:, where] for where in columns], axis=1)
                for ref in (own_ref, peer_ref)
            ],
            axis=0,
        )
        part = slice(i * block, (i + 1) * block)
        x0 = momentum_rate * momentum_ref[part].astype(f32) + tdot(toks, cots)
        x0 = x0.astype(bf16)
        x0_ref[part] = x0
        term = tdot(x0, x0)
        gram = term if gram is None else gram + term
    gram_ref[...] = gram.astype(bf16)


def update_kernel(model_width, order_ref, own_ref, peer_ref, x0_ref, weight_ref, *out_refs):
    gram = own_ref[...].astype(f32) + peer_ref[...].astype(f32)
    factor, remainder = update_matrix(gram)
    pieces = order_ref.shape[0]
    chunk, width = out_refs[0].shape
    for stage in range(STAGES):
        cols = slice(stage * width, (stage + 1) * width)
        for k in range(pieces):
            rows = pl.ds(pl.multiple_of(order_ref[k] * chunk, chunk), chunk)
            out_refs[stage * pieces + k][...] = renew(
                weight_ref[rows, cols],
                x0_ref[rows, :],
                x0_ref[rows, cols],
                factor,
                remainder[:, cols],
                model_width,
            )


def choose_kernel(half_ref, order_ref, own_ref, peer_ref, ids_ref, peer_ids_ref, *out_refs):
    _, rows, chunk = out_refs[0].shape
    half = half_ref[0]
    for rel, (ref, ids) in enumerate(((own_ref, ids_ref), (peer_ref, peer_ids_ref))):
        place = lax.broadcasted_iota(jnp.int32, (rows, rows), 0)
        pick = jnp.where(place == ids[...], 1.0, 0.0).astype(bf16)
        for k, out in enumerate(out_refs):
            for j in range(chunk // LANES):
                start = (2 * (order_ref[k] * (chunk // LANES) + j) + half) * LANES
                cols = ref[:, pl.ds(pl.multiple_of(start, LANES), LANES)]
                out[rel, :, j * LANES : (j + 1) * LANES] = tdot(pick, cols).astype(bf16)


def route_kernel(count, turn_ref, *refs):
    ins, outs, store = refs[:count], refs[count : 2 * count], refs[2 * count]
    for k in range(count):
        store[k] = ins[k][...]
    for k in range(count):
        outs[k][...] = store[turn_ref[0] ^ k]


def project_kernel(count, planes, which_ref, *refs):
    toks, weights = refs[:count], refs[count : count + planes]
    keep_ref, send_ref, store = refs[count + planes :]
    for k in range(planes):
        store[k] = weights[k][...]
    for k in range(count):
        for rel in range(2):
            got = jnp.dot(
                toks[k][rel], store[which_ref[2 * k + rel]], preferred_element_type=f32
            )
            if rel == 0:
                keep_ref[k] = got
            else:
                send_ref[k] = got.astype(bf16)


def join_kernel(count, keep_ref, other_ref, *out_refs):
    for k in range(count):
        out_refs[k][...] = (keep_ref[k] + other_ref[k].astype(f32)).astype(bf16)


def call(kernel, name, scalars, arrays, outs, scratch=()):
    return pl.pallas_call(
        kernel,
        out_shape=[pltpu.VMEM(shape, dtype) for shape, dtype in outs],
        in_specs=[pl.BlockSpec(memory_space=pltpu.SMEM)] * len(scalars)
        + [pl.BlockSpec(memory_space=pltpu.VMEM)] * len(arrays),
        out_specs=[pl.BlockSpec(memory_space=pltpu.VMEM)] * len(outs),
        scratch_shapes=list(scratch),
        compiler_params=pltpu.CompilerParams(vmem_limit_bytes=16 * 2**20),
        name=name,
    )(*scalars, *[pltpu.with_memory_space_constraint(a, pltpu.VMEM) for a in arrays])


def on_device(tokens, cotangent, weight_halves, momentum_halves, old_map, new_map, row_ids):
    slot_count = lax.axis_size("slot")
    group_count = lax.axis_size("group")
    planes = slot_count // 2
    hosts = slot_count // group_count
    slot = lax.axis_index("slot")
    half = slot % 2
    plane = slot // 2
    group = lax.axis_index("group")

    from_group = (group ^ jnp.arange(group_count)).astype(jnp.int32)
    wanted_slot = 2 * plane + (half ^ jnp.arange(2))
    experts = new_map[from_group[:, None], wanted_slot[None, :]]
    lists = old_map[wanted_slot // hosts]
    holder = jnp.argmax((lists[None] == experts[:, :, None]).astype(jnp.int32), axis=2)

    inputs = (tokens, cotangent, weight_halves[0], momentum_halves[0], row_ids)
    fits = group_count == planes and planes <= MOST_PERMUTES
    if fits and tokens.shape[1] == 2 * slot_count * LANES:
        return by_permutes(*inputs, from_group, holder)
    return by_all_to_all(*inputs, from_group, holder)


def by_permutes(tokens, cotangent, weight, momentum, row_ids, from_group, holder):
    slot_count = lax.axis_size("slot")
    count = lax.axis_size("group")
    planes = slot_count // 2
    row_count, model_width = tokens.shape
    hidden = cotangent.shape[1]
    half_rows = model_width // 2
    chunk = half_rows // count
    width = hidden // STAGES
    half = (lax.axis_index("slot") % 2).astype(jnp.int32)
    plane = (lax.axis_index("slot") // 2).astype(jnp.int32)
    group = lax.axis_index("group").astype(jnp.int32)
    half_of = half.reshape(1)

    peer_cot = swapped(cotangent)
    peer_tokens = swapped(tokens)
    peer_ids = swapped(row_ids)
    x0, own_gram = call(
        front_kernel,
        "front",
        [half_of],
        [tokens, peer_tokens, cotangent, peer_cot, momentum],
        [((half_rows, hidden), bf16), ((hidden, hidden), bf16)],
    )
    peer_gram = swapped(own_gram)

    token_cuts = call(
        choose_kernel,
        "choose",
        [half_of, from_group],
        [tokens, peer_tokens, row_ids, peer_ids],
        [((2, row_count, chunk), bf16)] * count,
    )

    pieces = call(
        functools.partial(update_kernel, model_width),
        "update",
        [from_group],
        [own_gram, peer_gram, x0, weight],
        [((chunk, width), bf16)] * (STAGES * count),
    )

    turn = (group ^ plane).reshape(1)
    routed = []
    for stage in range(STAGES):
        mine = pieces[stage * count : (stage + 1) * count]
        landed = [mine[0]] + [shifted(mine[k], "group", 1, k) for k in range(1, count)]
        if stage == STAGES - 1:
            token_cuts, landed = lax.optimization_barrier((token_cuts, landed))
        routed.append(
            call(
                functools.partial(route_kernel, count),
                "route",
                [turn],
                landed,
                [((chunk, width), bf16)] * count,
                [pltpu.VMEM((count, chunk, width), bf16)],
            )
        )
    arrived = []
    for stage in range(STAGES):
        mine = routed[stage]
        arrived.append([mine[0]] + [shifted(mine[k], "slot", 2, k) for k in range(1, planes)])

    requested = [token_cuts[0]] + [
        shifted(token_cuts[k], "group", 1, k) for k in range(1, count)
    ]
    which = (plane ^ holder.astype(jnp.int32)).reshape(-1)

    outputs = []
    for stage in range(STAGES):
        keep, send = call(
            functools.partial(project_kernel, count, planes),
            "project",
            [which],
            requested + arrived[stage],
            [((count, row_count, width), f32), ((count, row_count, width), bf16)],
            [pltpu.VMEM((planes, chunk, width), bf16)],
        )
        other = swapped(send)
        mine = call(
            functools.partial(join_kernel, count),
            "join",
            [],
            [keep, other],
            [((row_count, width), bf16)] * count,
        )
        returned = [mine[0]] + [shifted(mine[k], "group", 1, k) for k in range(1, count)]
        outputs.append(sum(r.astype(f32) for r in returned).astype(bf16))
    return jnp.concatenate(outputs, axis=1)


def by_all_to_all(tokens, cotangent, weight, momentum, row_ids, from_group, holder):
    slot_count = lax.axis_size("slot")
    group_count = lax.axis_size("group")
    planes = slot_count // 2
    owners = max(1, 2 * group_count // slot_count)
    row_count, model_width = tokens.shape
    hidden = cotangent.shape[1]
    half_rows = model_width // 2
    chunk = half_rows // group_count
    width = hidden // STAGES
    half = lax.axis_index("slot") % 2
    plane = lax.axis_index("slot") // 2
    group = lax.axis_index("group")

    peer_cot = swapped(cotangent)
    peer_tokens = swapped(pick_columns(tokens, 1 - half, slot_count))
    own_tokens = pick_columns(tokens, half, slot_count)
    gradient = tdot(own_tokens, cotangent) + tdot(peer_tokens, peer_cot)
    x0 = (momentum_rate * momentum.astype(f32) + gradient).astype(bf16)
    own_gram = tdot(x0, x0).astype(bf16)
    factor, remainder = update_matrix(own_gram.astype(f32) + swapped(own_gram).astype(f32))
    renewed = renew(weight, x0, x0, factor, remainder, model_width)

    pick = (row_ids[0][:, None] == jnp.arange(row_count)[None, :]).astype(bf16)
    chosen = jnp.dot(pick, tokens, preferred_element_type=f32).astype(bf16)
    own_chosen = pick_columns(chosen, half, slot_count)
    peer_chosen = swapped(pick_columns(chosen, 1 - half, slot_count))
    both = jnp.stack([own_chosen, peer_chosen]).reshape(2, row_count, group_count, chunk)
    requested = jnp.stack(exchange(lambda d: both[:, :, d], "group", 1))
    masked = jnp.stack(
        [jnp.where((holder == (plane ^ k))[:, :, None, None], requested, 0) for k in range(planes)]
    )

    outputs = []
    for stage in range(STAGES):
        cols = slice(stage * width, (stage + 1) * width)
        chunks = renewed[:, cols].reshape(group_count, chunk, width)
        in_plane = jnp.stack(exchange(lambda d: chunks[d], "group", 1))
        by_owner = jnp.take(in_plane, group ^ jnp.arange(group_count), axis=0)
        by_plane = by_owner.reshape(planes, owners, chunk, width)
        arrived = jnp.stack(exchange(lambda d: by_plane[d], "slot", 2))
        partial = [
            jnp.einsum(
                "pktc,pcw->ktw",
                masked[:, :, rel],
                jnp.take(arrived, (half ^ rel) * owners // 2, axis=1),
                preferred_element_type=f32,
            )
            for rel in range(2)
        ]
        other = swapped(partial[1].astype(bf16))
        summed = (partial[0] + other.astype(f32)).astype(bf16)
        by_group = jnp.take(summed, group ^ jnp.arange(group_count), axis=0)
        returned = exchange(lambda d: by_group[d], "group", 1)
        outputs.append(sum(r.astype(f32) for r in returned).astype(bf16))
    return jnp.concatenate(outputs, axis=1)


def solution(mesh):
    placed = (
        P(("group", "slot"), None),
        P(("group", "slot"), None),
        P(("group", "slot"), None, None),
        P(("group", "slot"), None, None),
        P(),
        P(),
        P(("group", "slot"), None),
    )
    return jax.shard_map(
        on_device, mesh=mesh, in_specs=placed, out_specs=P(("group", "slot"), None), check_vma=False
    )
```

```python
import functools
import math

import jax
import jax.numpy as jnp
from jax import lax
from jax.experimental import pallas as pl
from jax.experimental.pallas import tpu as pltpu
from jax.sharding import PartitionSpec as P


coef_a = 3.4445
coef_b = -4.775
coef_c = 2.0315
momentum_rate = 0.95
step_scale = 0.01
gram_eps = 1e-06
contract_rows = (((0,), (0,)), ((), ()))
STAGES = 2
MOST_PERMUTES = 4
LANES = 128
bf16 = jnp.bfloat16
f32 = jnp.float32


def shifted(shard, axis, stride, k):
    size = lax.axis_size(axis)
    return lax.ppermute(shard, axis, [(i, i ^ (k * stride)) for i in range(size)])


def swapped(shard):
    return shifted(shard, "slot", 1, 1)


def exchange(piece, axis, stride):
    size = lax.axis_size(axis)
    count = size // stride
    place = lax.axis_index(axis) // stride
    stacked = jnp.stack([piece(d) for d in range(count)])
    groups = [[first + stride * d for d in range(count)] for first in range(stride)]
    landed = lax.all_to_all(
        stacked,
        axis,
        split_axis=0,
        concat_axis=0,
        tiled=True,
        axis_index_groups=groups if stride > 1 else None,
    )
    return [lax.dynamic_index_in_dim(landed, place ^ k, 0, keepdims=False) for k in range(count)]


def pick_columns(token_block, which_half, slot_count):
    row_count, col_count = token_block.shape
    pieces_view = token_block.reshape(row_count, slot_count, 2, col_count // (2 * slot_count))
    chosen = lax.dynamic_index_in_dim(pieces_view, which_half, axis=2, keepdims=False)
    return chosen.reshape(row_count, col_count // 2)


def matmul(left, right):
    return jnp.dot(left.astype(bf16), right.astype(bf16), preferred_element_type=f32)


def tdot(left, right):
    return lax.dot_general(left, right, contract_rows, preferred_element_type=f32)


def update_matrix(gram):
    on_diagonal = lax.broadcasted_iota(jnp.int32, gram.shape, 0) == lax.broadcasted_iota(
        jnp.int32, gram.shape, 1
    )
    norm_sq = jnp.sum(jnp.where(on_diagonal, gram, 0.0), keepdims=True) + gram_eps
    first = gram * (1.0 / norm_sq)
    poly_first = coef_b * first + coef_c * matmul(first, first)
    half_way = coef_a * first + matmul(first, poly_first)
    second = coef_a * half_way + matmul(poly_first, half_way)
    poly_second = coef_b * second + coef_c * matmul(second, second)
    remainder = coef_a * (poly_first + poly_second) + matmul(poly_first, poly_second)
    return lax.rsqrt(norm_sq), remainder.astype(bf16)


def renew(weight, x0, x0_cols, factor, remainder, model_width):
    moved = coef_a * coef_a * x0_cols.astype(f32) + matmul(x0, remainder)
    scale = step_scale * math.sqrt(model_width) * factor
    return (weight.astype(f32) - scale * moved).astype(bf16)


def load_kernel(count, *refs):
    sources, targets, sems = refs[:count], refs[count : 2 * count], refs[2 * count]
    copies = [pltpu.make_async_copy(sources[i], targets[i], sems.at[i]) for i in range(count)]
    for copy in copies:
        copy.start()
    for copy in copies:
        copy.wait()


def own_place():
    slot = lax.axis_index("slot")
    return lax.axis_index("group"), lax.div(slot, 2), lax.rem(slot, 2)


def half_columns(ref, first, count, half):
    parts = []
    for j in range(count):
        start = (2 * (first + j) + half) * LANES
        parts.append(ref[:, pl.ds(pl.multiple_of(start, LANES), LANES)])
    return jnp.concatenate(parts, axis=1)


def front_kernel(own_ref, peer_ref, cot_ref, peer_cot_ref, momentum_ref, x0_ref, gram_ref):
    rows = x0_ref.shape[0]
    half = own_place()[2]
    cots = jnp.concatenate([cot_ref[...], peer_cot_ref[...]], axis=0)
    gram = None
    block = 2 * LANES
    for i in range(rows // block):
        toks = jnp.concatenate(
            [half_columns(ref, 2 * i, 2, half) for ref in (own_ref, peer_ref)], axis=0
        )
        part = slice(i * block, (i + 1) * block)
        x0 = momentum_rate * momentum_ref[part].astype(f32) + tdot(toks, cots)
        x0 = x0.astype(bf16)
        x0_ref[part] = x0
        term = tdot(x0, x0)
        gram = term if gram is None else gram + term
    gram_ref[...] = gram.astype(bf16)


def renew_pieces(model_width, stage, x0_ref, weight_ref, factor, remainder, out_refs):
    group = own_place()[0]
    chunk, width = out_refs[0].shape
    cols = slice(stage * width, (stage + 1) * width)
    for k in range(len(out_refs)):
        rows = pl.ds(pl.multiple_of((group ^ k) * chunk, chunk), chunk)
        out_refs[k][...] = renew(
            weight_ref[rows, cols],
            x0_ref[rows, :],
            x0_ref[rows, cols],
            factor,
            remainder,
            model_width,
        )


def update_kernel(model_width, own_ref, peer_ref, x0_ref, weight_ref, remainder_ref, factor_ref, *out_refs):
    gram = own_ref[...].astype(f32) + peer_ref[...].astype(f32)
    factor, remainder = update_matrix(gram)
    remainder_ref[...] = remainder
    factor_ref[...] = jnp.broadcast_to(factor, factor_ref.shape)
    width = out_refs[0].shape[1]
    renew_pieces(model_width, 0, x0_ref, weight_ref, factor, remainder[:, :width], out_refs)


def later_kernel(model_width, stage, remainder_ref, factor_ref, x0_ref, weight_ref, *out_refs):
    width = out_refs[0].shape[1]
    remainder = remainder_ref[:, stage * width : (stage + 1) * width]
    renew_pieces(
        model_width, stage, x0_ref, weight_ref, factor_ref[:1, :1], remainder, out_refs
    )


def choose_kernel(
    hosts, old_ref, new_ref, own_ref, peer_ref, ids_ref, peer_ids_ref, which_ref, *out_refs
):
    _, rows, chunk = out_refs[0].shape
    group, plane, half = own_place()
    planes = old_ref.shape[1]
    for k in range(len(out_refs)):
        for rel in range(2):
            wanted_slot = 2 * plane + (half ^ rel)
            owner = lax.div(wanted_slot, hosts)
            expert = new_ref[group ^ k, wanted_slot]
            holder = jnp.int32(0)
            for p in range(planes):
                holder = jnp.where(old_ref[owner, p] == expert, p, holder)
            which_ref[2 * k + rel] = plane ^ holder
    for rel, (ref, ids) in enumerate(((own_ref, ids_ref), (peer_ref, peer_ids_ref))):
        place = lax.broadcasted_iota(jnp.int32, (rows, rows), 0)
        pick = jnp.where(place == ids[...], 1.0, 0.0).astype(bf16)
        for k, out in enumerate(out_refs):
            count = chunk // LANES
            cols = half_columns(ref, (group ^ k) * count, count, half)
            out[rel] = tdot(pick, cols).astype(bf16)


def route_kernel(count, *refs):
    ins, outs, store = refs[:count], refs[count : 2 * count], refs[2 * count]
    group, plane, _ = own_place()
    for k in range(count):
        store[k] = ins[k][...]
    for k in range(count):
        outs[k][...] = store[group ^ plane ^ k]


def project_kernel(count, planes, which_ref, *refs):
    toks, weights = refs[:count], refs[count : count + planes]
    keep_ref, send_ref, store = refs[count + planes :]
    for k in range(planes):
        store[k] = weights[k][...]
    for rel in (1, 0):
        for k in range(count):
            got = jnp.dot(
                toks[k][rel], store[which_ref[2 * k + rel]], preferred_element_type=f32
            )
            if rel == 0:
                keep_ref[k] = got
            else:
                send_ref[k] = got.astype(bf16)


def join_kernel(count, keep_ref, other_ref, *out_refs):
    for k in range(count):
        out_refs[k][...] = (keep_ref[k] + other_ref[k].astype(f32)).astype(bf16)


def finish_kernel(count, *refs):
    out_ref = refs[-1]
    width = refs[0].shape[1]
    for stage in range(STAGES):
        parts = [r[...].astype(f32) for r in refs[stage * count : (stage + 1) * count]]
        out_ref[:, stage * width : (stage + 1) * width] = sum(parts).astype(out_ref.dtype)


VMEM, SMEM, HBM = pltpu.VMEM, pltpu.SMEM, pltpu.HBM


def call(kernel, arrays, outs, scratch=(), spaces=None, out_spaces=None):
    spaces = spaces or [VMEM] * len(arrays)
    out_spaces = out_spaces or [VMEM] * len(outs)
    made = {
        VMEM: lambda shape, dtype: pltpu.VMEM(shape, dtype),
        SMEM: lambda shape, dtype: pltpu.SMEM(shape, dtype),
        None: jax.ShapeDtypeStruct,
    }
    return pl.pallas_call(
        kernel,
        out_shape=[made[where](*out) for where, out in zip(out_spaces, outs)],
        in_specs=[pl.BlockSpec(memory_space=where or SMEM) for where in spaces],
        out_specs=[pl.BlockSpec(memory_space=where or VMEM) for where in out_spaces],
        scratch_shapes=list(scratch),
        compiler_params=pltpu.CompilerParams(vmem_limit_bytes=16 * 2**20),
    )(
        *[
            a if where is None else pltpu.with_memory_space_constraint(a, where)
            for where, a in zip(spaces, arrays)
        ]
    )


def on_device(tokens, cotangent, weight_halves, momentum_halves, old_map, new_map, row_ids):
    slot_count = lax.axis_size("slot")
    group_count = lax.axis_size("group")
    planes = slot_count // 2
    inputs = (
        tokens,
        cotangent,
        weight_halves[0],
        momentum_halves[0],
        old_map,
        new_map,
        row_ids,
    )
    fits = group_count == planes and planes <= MOST_PERMUTES
    if fits and tokens.shape[1] == 2 * slot_count * LANES:
        return by_permutes(*inputs)
    return by_all_to_all(*inputs)


FIRST = (3, 1, 2)
ACROSS = (3, 2, 1)


def spread(mine, axis, stride, order):
    landed = [mine[0]] + [None] * (len(mine) - 1)
    for k in order:
        if k < len(mine):
            landed[k] = shifted(mine[k], axis, stride, k)
    return landed


def by_permutes(tokens, cotangent, weight, momentum, old_map, new_map, row_ids):
    slot_count = lax.axis_size("slot")
    count = lax.axis_size("group")
    planes = slot_count // 2
    hosts = slot_count // count
    row_count, model_width = tokens.shape
    hidden = cotangent.shape[1]
    half_rows = model_width // 2
    chunk = half_rows // count
    width = hidden // STAGES

    peer_tokens = swapped(tokens)
    peer_cot = swapped(cotangent)
    to_load = [tokens, cotangent, momentum, weight, row_ids]
    tokens_in, cot_in, momentum_in, weight_in, ids_in = call(
        functools.partial(load_kernel, len(to_load)),
        to_load,
        [(a.shape, a.dtype) for a in to_load],
        [pltpu.SemaphoreType.DMA((len(to_load),))],
        spaces=[HBM] * len(to_load),
    )
    x0, own_gram = call(
        front_kernel,
        [tokens_in, peer_tokens, cot_in, peer_cot, momentum_in],
        [((half_rows, hidden), bf16), ((hidden, hidden), bf16)],
    )
    peer_gram = swapped(own_gram)
    peer_ids = swapped(row_ids)

    which, *token_cuts = call(
        functools.partial(choose_kernel, hosts),
        [old_map, new_map, tokens_in, peer_tokens, ids_in, peer_ids],
        [((2 * count,), jnp.int32)] + [((2, row_count, chunk), bf16)] * count,
        spaces=[None, None] + [VMEM] * 4,
        out_spaces=[SMEM] + [VMEM] * count,
    )

    remainder, factor, *first_pieces = call(
        functools.partial(update_kernel, model_width),
        [own_gram, peer_gram, x0, weight_in],
        [((hidden, hidden), bf16), ((8, LANES), f32)] + [((chunk, width), bf16)] * count,
    )
    arrived = []
    for stage in range(STAGES):
        pieces = first_pieces
        if stage:
            pieces = call(
                functools.partial(later_kernel, model_width, stage),
                [remainder, factor, x0, weight_in],
                [((chunk, width), bf16)] * count,
            )
        landed = spread(pieces, "group", 1, FIRST)
        routed = call(
            functools.partial(route_kernel, count),
            landed,
            [((chunk, width), bf16)] * count,
            [pltpu.VMEM((count, chunk, width), bf16)],
        )
        arrived.append(spread(routed, "slot", 2, ACROSS))

    requested = spread(token_cuts, "group", 1, FIRST)

    returned = []
    for stage in range(STAGES):
        keep, send = call(
            functools.partial(project_kernel, count, planes),
            [which] + requested + arrived[stage],
            [((count, row_count, width), f32), ((count, row_count, width), bf16)],
            [pltpu.VMEM((planes, chunk, width), bf16)],
            spaces=[SMEM] + [VMEM] * (count + planes),
        )
        other = swapped(send)
        mine = call(
            functools.partial(join_kernel, count),
            [keep, other],
            [((row_count, width), bf16)] * count,
        )
        returned += spread(mine, "group", 1, FIRST)
    return call(
        functools.partial(finish_kernel, count),
        returned,
        [((row_count, hidden), bf16)],
        out_spaces=[None],
    )[0]


def by_all_to_all(tokens, cotangent, weight, momentum, old_map, new_map, row_ids):
    slot_count = lax.axis_size("slot")
    group_count = lax.axis_size("group")
    planes = slot_count // 2
    owners = max(1, 2 * group_count // slot_count)
    row_count, model_width = tokens.shape
    hidden = cotangent.shape[1]
    half_rows = model_width // 2
    chunk = half_rows // group_count
    width = hidden // STAGES
    half = lax.axis_index("slot") % 2
    plane = lax.axis_index("slot") // 2
    group = lax.axis_index("group")
    hosts = slot_count // group_count

    from_group = group ^ jnp.arange(group_count)
    wanted_slot = 2 * plane + (half ^ jnp.arange(2))
    experts = new_map[from_group[:, None], wanted_slot[None, :]]
    lists = old_map[wanted_slot // hosts]
    holder = jnp.argmax((lists[None] == experts[:, :, None]).astype(jnp.int32), axis=2)

    peer_cot = swapped(cotangent)
    peer_tokens = swapped(pick_columns(tokens, 1 - half, slot_count))
    own_tokens = pick_columns(tokens, half, slot_count)
    gradient = tdot(own_tokens, cotangent) + tdot(peer_tokens, peer_cot)
    x0 = (momentum_rate * momentum.astype(f32) + gradient).astype(bf16)
    own_gram = tdot(x0, x0).astype(bf16)
    factor, remainder = update_matrix(own_gram.astype(f32) + swapped(own_gram).astype(f32))
    renewed = renew(weight, x0, x0, factor, remainder, model_width)

    pick = (row_ids[0][:, None] == jnp.arange(row_count)[None, :]).astype(bf16)
    chosen = jnp.dot(pick, tokens, preferred_element_type=f32).astype(bf16)
    own_chosen = pick_columns(chosen, half, slot_count)
    peer_chosen = swapped(pick_columns(chosen, 1 - half, slot_count))
    both = jnp.stack([own_chosen, peer_chosen]).reshape(2, row_count, group_count, chunk)
    requested = jnp.stack(exchange(lambda d: both[:, :, d], "group", 1))
    outputs = []
    for stage in range(STAGES):
        cols = slice(stage * width, (stage + 1) * width)
        chunks = renewed[:, cols].reshape(group_count, chunk, width)
        in_plane = jnp.stack(exchange(lambda d: chunks[d], "group", 1))
        by_owner = jnp.take(in_plane, group ^ jnp.arange(group_count), axis=0)
        by_plane = by_owner.reshape(planes, owners, chunk, width)
        arrived = jnp.stack(exchange(lambda d: by_plane[d], "slot", 2))
        partial = [
            jnp.einsum(
                "ktc,kcw->ktw",
                requested[:, rel],
                arrived[plane ^ holder[:, rel], (half ^ rel) * owners // 2],
                preferred_element_type=f32,
            )
            for rel in range(2)
        ]
        other = swapped(partial[1].astype(bf16))
        summed = (partial[0] + other.astype(f32)).astype(bf16)
        by_group = jnp.take(summed, group ^ jnp.arange(group_count), axis=0)
        returned = exchange(lambda d: by_group[d], "group", 1)
        outputs.append(sum(r.astype(f32) for r in returned).astype(bf16))
    return jnp.concatenate(outputs, axis=1)


def solution(mesh):
    placed = (
        P(("group", "slot"), None),
        P(("group", "slot"), None),
        P(("group", "slot"), None, None),
        P(("group", "slot"), None, None),
        P(),
        P(),
        P(("group", "slot"), None),
    )
    return jax.shard_map(
        on_device, mesh=mesh, in_specs=placed, out_specs=P(("group", "slot"), None), check_vma=False
    )
```

```python
import functools
import math

import jax
import jax.numpy as jnp
from jax import lax
from jax.experimental import pallas as pl
from jax.experimental.pallas import tpu as pltpu
from jax.sharding import PartitionSpec as P


coef_a = 3.4445
coef_b = -4.775
coef_c = 2.0315
momentum_rate = 0.95
step_scale = 0.01
gram_eps = 1e-06
contract_rows = (((0,), (0,)), ((), ()))
WIDTHS = (1, 2, 1)
TAILS = ((0, 1), (2,))
MOST_PERMUTES = 4
LANES = 128
bf16 = jnp.bfloat16
f32 = jnp.float32


def shifted(shard, axis, stride, k):
    size = lax.axis_size(axis)
    return lax.ppermute(shard, axis, [(i, i ^ (k * stride)) for i in range(size)])


def swapped(shard):
    return shifted(shard, "slot", 1, 1)


def exchange(piece, axis, stride):
    size = lax.axis_size(axis)
    count = size // stride
    place = lax.axis_index(axis) // stride
    stacked = jnp.stack([piece(d) for d in range(count)])
    groups = [[first + stride * d for d in range(count)] for first in range(stride)]
    landed = lax.all_to_all(
        stacked,
        axis,
        split_axis=0,
        concat_axis=0,
        tiled=True,
        axis_index_groups=groups if stride > 1 else None,
    )
    return [lax.dynamic_index_in_dim(landed, place ^ k, 0, keepdims=False) for k in range(count)]


def pick_columns(token_block, which_half, slot_count):
    row_count, col_count = token_block.shape
    pieces_view = token_block.reshape(row_count, slot_count, 2, col_count // (2 * slot_count))
    chosen = lax.dynamic_index_in_dim(pieces_view, which_half, axis=2, keepdims=False)
    return chosen.reshape(row_count, col_count // 2)


def matmul(left, right):
    return jnp.dot(left.astype(bf16), right.astype(bf16), preferred_element_type=f32)


def tdot(left, right):
    return lax.dot_general(left, right, contract_rows, preferred_element_type=f32)


def update_matrix(gram):
    on_diagonal = lax.broadcasted_iota(jnp.int32, gram.shape, 0) == lax.broadcasted_iota(
        jnp.int32, gram.shape, 1
    )
    norm_sq = jnp.sum(jnp.where(on_diagonal, gram, 0.0), keepdims=True) + gram_eps
    first = gram * (1.0 / norm_sq)
    poly_first = coef_b * first + coef_c * matmul(first, first)
    half_way = coef_a * first + matmul(first, poly_first)
    second = coef_a * half_way + matmul(poly_first, half_way)
    poly_second = coef_b * second + coef_c * matmul(second, second)
    remainder = coef_a * (poly_first + poly_second) + matmul(poly_first, poly_second)
    return lax.rsqrt(norm_sq), remainder.astype(bf16)


def renew(weight, x0, x0_cols, factor, remainder, model_width):
    moved = coef_a * coef_a * x0_cols.astype(f32) + matmul(x0, remainder)
    scale = step_scale * math.sqrt(model_width) * factor
    return (weight.astype(f32) - scale * moved).astype(bf16)


def load_kernel(count, *refs):
    sources, targets, sems = refs[:count], refs[count : 2 * count], refs[2 * count]
    copies = [pltpu.make_async_copy(sources[i], targets[i], sems.at[i]) for i in range(count)]
    for copy in copies:
        copy.start()
    for copy in copies:
        copy.wait()


def own_place():
    slot = lax.axis_index("slot")
    return lax.axis_index("group"), lax.div(slot, 2), lax.rem(slot, 2)


def half_columns(ref, first, count, half):
    parts = []
    for j in range(count):
        start = (2 * (first + j) + half) * LANES
        parts.append(ref[:, pl.ds(pl.multiple_of(start, LANES), LANES)])
    return jnp.concatenate(parts, axis=1)


def front_kernel(own_ref, peer_ref, cot_ref, peer_cot_ref, momentum_ref, x0_ref, gram_ref):
    rows = x0_ref.shape[0]
    half = own_place()[2]
    cots = jnp.concatenate([cot_ref[...], peer_cot_ref[...]], axis=0)
    gram = None
    block = 2 * LANES
    for i in range(rows // block):
        toks = jnp.concatenate(
            [half_columns(ref, 2 * i, 2, half) for ref in (own_ref, peer_ref)], axis=0
        )
        part = slice(i * block, (i + 1) * block)
        x0 = momentum_rate * momentum_ref[part].astype(f32) + tdot(toks, cots)
        x0 = x0.astype(bf16)
        x0_ref[part] = x0
        term = tdot(x0, x0)
        gram = term if gram is None else gram + term
    gram_ref[...] = gram.astype(bf16)


def stage_columns(hidden):
    unit = hidden // sum(WIDTHS)
    starts = [unit * sum(WIDTHS[:i]) for i in range(len(WIDTHS))]
    return [slice(start, start + unit * share) for start, share in zip(starts, WIDTHS)]


def renew_pieces(model_width, cols, x0_ref, weight_ref, factor, remainder, out_refs):
    group = own_place()[0]
    chunk = out_refs[0].shape[0]
    for k in range(len(out_refs)):
        rows = pl.ds(pl.multiple_of((group ^ k) * chunk, chunk), chunk)
        out_refs[k][...] = renew(
            weight_ref[rows, cols],
            x0_ref[rows, :],
            x0_ref[rows, cols],
            factor,
            remainder,
            model_width,
        )


def update_kernel(
    model_width, cols, own_ref, peer_ref, x0_ref, weight_ref, remainder_ref, factor_ref, *out_refs
):
    gram = own_ref[...].astype(f32) + peer_ref[...].astype(f32)
    factor, remainder = update_matrix(gram)
    remainder_ref[...] = remainder
    factor_ref[...] = jnp.broadcast_to(factor, factor_ref.shape)
    renew_pieces(model_width, cols, x0_ref, weight_ref, factor, remainder[:, cols], out_refs)


def later_kernel(model_width, cols, remainder_ref, factor_ref, x0_ref, weight_ref, *out_refs):
    remainder = remainder_ref[:, cols]
    renew_pieces(model_width, cols, x0_ref, weight_ref, factor_ref[:1, :1], remainder, out_refs)


def choose_kernel(
    hosts, old_ref, new_ref, own_ref, peer_ref, ids_ref, peer_ids_ref, which_ref, *out_refs
):
    _, rows, chunk = out_refs[0].shape
    group, plane, half = own_place()
    planes = old_ref.shape[1]
    for k in range(len(out_refs)):
        for rel in range(2):
            wanted_slot = 2 * plane + (half ^ rel)
            owner = lax.div(wanted_slot, hosts)
            expert = new_ref[group ^ k, wanted_slot]
            holder = jnp.int32(0)
            for p in range(planes):
                holder = jnp.where(old_ref[owner, p] == expert, p, holder)
            which_ref[2 * k + rel] = plane ^ holder
    for rel, (ref, ids) in enumerate(((own_ref, ids_ref), (peer_ref, peer_ids_ref))):
        place = lax.broadcasted_iota(jnp.int32, (rows, rows), 0)
        pick = jnp.where(place == ids[...], 1.0, 0.0).astype(bf16)
        for k, out in enumerate(out_refs):
            count = chunk // LANES
            cols = half_columns(ref, (group ^ k) * count, count, half)
            out[rel] = tdot(pick, cols).astype(bf16)


def route_kernel(count, *refs):
    ins, outs, store = refs[:count], refs[count : 2 * count], refs[2 * count]
    group, plane, _ = own_place()
    for k in range(count):
        store[k] = ins[k][...]
    for k in range(count):
        outs[k][...] = store[group ^ plane ^ k]


def project_kernel(count, planes, stages, which_ref, *refs):
    toks, weights = refs[:count], refs[count : count + planes * stages]
    keep_ref, send_ref = refs[count + planes * stages :][:2]
    stores = refs[count + planes * stages + 2 :]
    for stage in range(stages):
        for k in range(planes):
            stores[stage][k] = weights[stage * planes + k][...]
    for rel in (1, 0):
        for k in range(count):
            place = which_ref[2 * k + rel]
            start = 0
            for store in stores:
                cols = slice(start, start + store.shape[2])
                start = cols.stop
                got = jnp.dot(toks[k][rel], store[place], preferred_element_type=f32)
                if rel == 0:
                    keep_ref[k, :, cols] = got
                else:
                    send_ref[k, :, cols] = got.astype(bf16)


def join_kernel(count, keep_ref, other_ref, *out_refs):
    for k in range(count):
        out_refs[k][...] = (keep_ref[k] + other_ref[k].astype(f32)).astype(bf16)


def finish_kernel(count, *refs):
    out_ref = refs[-1]
    start = 0
    for tail in range(len(TAILS)):
        mine = refs[tail * count : (tail + 1) * count]
        cols = slice(start, start + mine[0].shape[1])
        start = cols.stop
        out_ref[:, cols] = sum(r[...].astype(f32) for r in mine).astype(out_ref.dtype)


VMEM, SMEM, HBM = pltpu.VMEM, pltpu.SMEM, pltpu.HBM


def call(kernel, arrays, outs, scratch=(), spaces=None, out_spaces=None):
    spaces = spaces or [VMEM] * len(arrays)
    out_spaces = out_spaces or [VMEM] * len(outs)
    made = {
        VMEM: lambda shape, dtype: pltpu.VMEM(shape, dtype),
        SMEM: lambda shape, dtype: pltpu.SMEM(shape, dtype),
        None: jax.ShapeDtypeStruct,
    }
    return pl.pallas_call(
        kernel,
        out_shape=[made[where](*out) for where, out in zip(out_spaces, outs)],
        in_specs=[pl.BlockSpec(memory_space=where or SMEM) for where in spaces],
        out_specs=[pl.BlockSpec(memory_space=where or VMEM) for where in out_spaces],
        scratch_shapes=list(scratch),
        compiler_params=pltpu.CompilerParams(vmem_limit_bytes=16 * 2**20),
    )(
        *[
            a if where is None else pltpu.with_memory_space_constraint(a, where)
            for where, a in zip(spaces, arrays)
        ]
    )


def on_device(tokens, cotangent, weight_halves, momentum_halves, old_map, new_map, row_ids):
    slot_count = lax.axis_size("slot")
    group_count = lax.axis_size("group")
    planes = slot_count // 2
    inputs = (
        tokens,
        cotangent,
        weight_halves[0],
        momentum_halves[0],
        old_map,
        new_map,
        row_ids,
    )
    fits = group_count == planes and planes <= MOST_PERMUTES
    if fits and tokens.shape[1] == 2 * slot_count * LANES:
        return by_permutes(*inputs)
    return by_all_to_all(*inputs)


FIRST = (3, 1, 2)
ACROSS = (3, 2, 1)


def spread(mine, axis, stride, order):
    landed = [mine[0]] + [None] * (len(mine) - 1)
    for k in order:
        if k < len(mine):
            landed[k] = shifted(mine[k], axis, stride, k)
    return landed


def by_permutes(tokens, cotangent, weight, momentum, old_map, new_map, row_ids):
    slot_count = lax.axis_size("slot")
    count = lax.axis_size("group")
    planes = slot_count // 2
    hosts = slot_count // count
    row_count, model_width = tokens.shape
    hidden = cotangent.shape[1]
    half_rows = model_width // 2
    chunk = half_rows // count
    columns = stage_columns(hidden)

    peer_tokens = swapped(tokens)
    peer_cot = swapped(cotangent)
    peer_ids = swapped(row_ids)
    to_load = [tokens, cotangent, momentum, weight, row_ids]
    tokens_in, cot_in, momentum_in, weight_in, ids_in = call(
        functools.partial(load_kernel, len(to_load)),
        to_load,
        [(a.shape, a.dtype) for a in to_load],
        [pltpu.SemaphoreType.DMA((len(to_load),))],
        spaces=[HBM] * len(to_load),
    )
    x0, own_gram = call(
        front_kernel,
        [tokens_in, peer_tokens, cot_in, peer_cot, momentum_in],
        [((half_rows, hidden), bf16), ((hidden, hidden), bf16)],
    )
    peer_gram = swapped(own_gram)

    which, *token_cuts = call(
        functools.partial(choose_kernel, hosts),
        [old_map, new_map, tokens_in, peer_tokens, ids_in, peer_ids],
        [((2 * count,), jnp.int32)] + [((2, row_count, chunk), bf16)] * count,
        spaces=[None, None] + [VMEM] * 4,
        out_spaces=[SMEM] + [VMEM] * count,
    )

    arrived = []
    for stage, cols in enumerate(columns):
        width = cols.stop - cols.start
        if stage == 0:
            remainder, factor, *pieces = call(
                functools.partial(update_kernel, model_width, cols),
                [own_gram, peer_gram, x0, weight_in],
                [((hidden, hidden), bf16), ((8, LANES), f32)] + [((chunk, width), bf16)] * count,
            )
        else:
            pieces = call(
                functools.partial(later_kernel, model_width, cols),
                [remainder, factor, x0, weight_in],
                [((chunk, width), bf16)] * count,
            )
        landed = spread(pieces, "group", 1, FIRST)
        routed = call(
            functools.partial(route_kernel, count),
            landed,
            [((chunk, width), bf16)] * count,
            [pltpu.VMEM((count, chunk, width), bf16)],
        )
        arrived.append(spread(routed, "slot", 2, ACROSS))

    requested = spread(token_cuts, "group", 1, FIRST)

    returned = []
    for stages in TAILS:
        widths = [columns[i].stop - columns[i].start for i in stages]
        keep, send = call(
            functools.partial(project_kernel, count, planes, len(stages)),
            [which] + requested + sum((arrived[i] for i in stages), []),
            [((count, row_count, sum(widths)), f32), ((count, row_count, sum(widths)), bf16)],
            [pltpu.VMEM((planes, chunk, width), bf16) for width in widths],
            spaces=[SMEM] + [VMEM] * (count + planes * len(stages)),
        )
        other = swapped(send)
        mine = call(
            functools.partial(join_kernel, count),
            [keep, other],
            [((row_count, sum(widths)), bf16)] * count,
        )
        returned += spread(mine, "group", 1, FIRST)
    return call(
        functools.partial(finish_kernel, count),
        returned,
        [((row_count, hidden), bf16)],
        out_spaces=[None],
    )[0]


def by_all_to_all(tokens, cotangent, weight, momentum, old_map, new_map, row_ids):
    slot_count = lax.axis_size("slot")
    group_count = lax.axis_size("group")
    planes = slot_count // 2
    owners = max(1, 2 * group_count // slot_count)
    row_count, model_width = tokens.shape
    hidden = cotangent.shape[1]
    half_rows = model_width // 2
    chunk = half_rows // group_count
    half = lax.axis_index("slot") % 2
    plane = lax.axis_index("slot") // 2
    group = lax.axis_index("group")
    hosts = slot_count // group_count

    from_group = group ^ jnp.arange(group_count)
    wanted_slot = 2 * plane + (half ^ jnp.arange(2))
    experts = new_map[from_group[:, None], wanted_slot[None, :]]
    lists = old_map[wanted_slot // hosts]
    holder = jnp.argmax((lists[None] == experts[:, :, None]).astype(jnp.int32), axis=2)

    peer_cot = swapped(cotangent)
    peer_tokens = swapped(pick_columns(tokens, 1 - half, slot_count))
    own_tokens = pick_columns(tokens, half, slot_count)
    gradient = tdot(own_tokens, cotangent) + tdot(peer_tokens, peer_cot)
    x0 = (momentum_rate * momentum.astype(f32) + gradient).astype(bf16)
    own_gram = tdot(x0, x0).astype(bf16)
    factor, remainder = update_matrix(own_gram.astype(f32) + swapped(own_gram).astype(f32))
    renewed = renew(weight, x0, x0, factor, remainder, model_width)

    pick = (row_ids[0][:, None] == jnp.arange(row_count)[None, :]).astype(bf16)
    chosen = jnp.dot(pick, tokens, preferred_element_type=f32).astype(bf16)
    own_chosen = pick_columns(chosen, half, slot_count)
    peer_chosen = swapped(pick_columns(chosen, 1 - half, slot_count))
    both = jnp.stack([own_chosen, peer_chosen]).reshape(2, row_count, group_count, chunk)
    requested = jnp.stack(exchange(lambda d: both[:, :, d], "group", 1))
    outputs = []
    for cols in (slice(0, hidden // 2), slice(hidden // 2, hidden)):
        width = cols.stop - cols.start
        chunks = renewed[:, cols].reshape(group_count, chunk, width)
        in_plane = jnp.stack(exchange(lambda d: chunks[d], "group", 1))
        by_owner = jnp.take(in_plane, group ^ jnp.arange(group_count), axis=0)
        by_plane = by_owner.reshape(planes, owners, chunk, width)
        arrived = jnp.stack(exchange(lambda d: by_plane[d], "slot", 2))
        partial = [
            jnp.einsum(
                "ktc,kcw->ktw",
                requested[:, rel],
                arrived[plane ^ holder[:, rel], (half ^ rel) * owners // 2],
                preferred_element_type=f32,
            )
            for rel in range(2)
        ]
        other = swapped(partial[1].astype(bf16))
        summed = (partial[0] + other.astype(f32)).astype(bf16)
        by_group = jnp.take(summed, group ^ jnp.arange(group_count), axis=0)
        returned = exchange(lambda d: by_group[d], "group", 1)
        outputs.append(sum(r.astype(f32) for r in returned).astype(bf16))
    return jnp.concatenate(outputs, axis=1)


def solution(mesh):
    placed = (
        P(("group", "slot"), None),
        P(("group", "slot"), None),
        P(("group", "slot"), None, None),
        P(("group", "slot"), None, None),
        P(),
        P(),
        P(("group", "slot"), None),
    )
    return jax.shard_map(
        on_device, mesh=mesh, in_specs=placed, out_specs=P(("group", "slot"), None), check_vma=False
    )
```

```python
import functools
import math

import jax
import jax.numpy as jnp
from jax import lax
from jax.experimental import pallas as pl
from jax.experimental.pallas import tpu as pltpu
from jax.sharding import PartitionSpec as P


coef_a = 3.4445
coef_b = -4.775
coef_c = 2.0315
momentum_rate = 0.95
step_scale = 0.01
gram_eps = 1e-06
contract_rows = (((0,), (0,)), ((), ()))
WIDTHS = (1, 1)
TAILS = ((0,), (1,))
MOST_PERMUTES = 4
LANES = 128
bf16 = jnp.bfloat16
f32 = jnp.float32


def shifted(shard, axis, stride, k):
    size = lax.axis_size(axis)
    return lax.ppermute(shard, axis, [(i, i ^ (k * stride)) for i in range(size)])


def swapped(shard):
    return shifted(shard, "slot", 1, 1)


def exchange(piece, axis, stride):
    size = lax.axis_size(axis)
    count = size // stride
    place = lax.axis_index(axis) // stride
    stacked = jnp.stack([piece(d) for d in range(count)])
    groups = [[first + stride * d for d in range(count)] for first in range(stride)]
    landed = lax.all_to_all(
        stacked,
        axis,
        split_axis=0,
        concat_axis=0,
        tiled=True,
        axis_index_groups=groups if stride > 1 else None,
    )
    return [lax.dynamic_index_in_dim(landed, place ^ k, 0, keepdims=False) for k in range(count)]


def pick_columns(token_block, which_half, slot_count):
    row_count, col_count = token_block.shape
    pieces_view = token_block.reshape(row_count, slot_count, 2, col_count // (2 * slot_count))
    chosen = lax.dynamic_index_in_dim(pieces_view, which_half, axis=2, keepdims=False)
    return chosen.reshape(row_count, col_count // 2)


def matmul(left, right):
    return jnp.dot(left.astype(bf16), right.astype(bf16), preferred_element_type=f32)


def tdot(left, right):
    return lax.dot_general(left, right, contract_rows, preferred_element_type=f32)


def update_matrix(gram):
    on_diagonal = lax.broadcasted_iota(jnp.int32, gram.shape, 0) == lax.broadcasted_iota(
        jnp.int32, gram.shape, 1
    )
    norm_sq = jnp.sum(jnp.where(on_diagonal, gram, 0.0), keepdims=True) + gram_eps
    first = gram * (1.0 / norm_sq)
    poly_first = coef_b * first + coef_c * matmul(first, first)
    half_way = coef_a * first + matmul(first, poly_first)
    second = coef_a * half_way + matmul(poly_first, half_way)
    poly_second = coef_b * second + coef_c * matmul(second, second)
    remainder = coef_a * (poly_first + poly_second) + matmul(poly_first, poly_second)
    return lax.rsqrt(norm_sq), remainder.astype(bf16)


def renew(weight, x0, x0_cols, factor, remainder, model_width):
    moved = coef_a * coef_a * x0_cols.astype(f32) + matmul(x0, remainder)
    scale = step_scale * math.sqrt(model_width) * factor
    return (weight.astype(f32) - scale * moved).astype(bf16)


def load_kernel(count, *refs):
    sources, targets, sems = refs[:count], refs[count : 2 * count], refs[2 * count]
    copies = [pltpu.make_async_copy(sources[i], targets[i], sems.at[i]) for i in range(count)]
    for copy in copies:
        copy.start()
    for copy in copies:
        copy.wait()


def own_place():
    slot = lax.axis_index("slot")
    return lax.axis_index("group"), lax.div(slot, 2), lax.rem(slot, 2)


def half_columns(ref, first, count, half):
    parts = []
    for j in range(count):
        start = (2 * (first + j) + half) * LANES
        parts.append(ref[:, pl.ds(pl.multiple_of(start, LANES), LANES)])
    return jnp.concatenate(parts, axis=1)


def front_kernel(own_ref, peer_ref, cot_ref, peer_cot_ref, momentum_ref, x0_ref, gram_ref):
    rows = x0_ref.shape[0]
    half = own_place()[2]
    cots = jnp.concatenate([cot_ref[...], peer_cot_ref[...]], axis=0)
    gram = None
    block = 2 * LANES
    for i in range(rows // block):
        toks = jnp.concatenate(
            [half_columns(ref, 2 * i, 2, half) for ref in (own_ref, peer_ref)], axis=0
        )
        part = slice(i * block, (i + 1) * block)
        x0 = momentum_rate * momentum_ref[part].astype(f32) + tdot(toks, cots)
        x0 = x0.astype(bf16)
        x0_ref[part] = x0
        term = tdot(x0, x0)
        gram = term if gram is None else gram + term
    gram_ref[...] = gram.astype(bf16)


def stage_columns(hidden):
    unit = hidden // sum(WIDTHS)
    starts = [unit * sum(WIDTHS[:i]) for i in range(len(WIDTHS))]
    return [slice(start, start + unit * share) for start, share in zip(starts, WIDTHS)]


def renew_pieces(model_width, cols, x0_ref, weight_ref, factor, remainder, out_refs):
    group = own_place()[0]
    chunk = out_refs[0].shape[0]
    for k in range(len(out_refs)):
        rows = pl.ds(pl.multiple_of((group ^ k) * chunk, chunk), chunk)
        out_refs[k][...] = renew(
            weight_ref[rows, cols],
            x0_ref[rows, :],
            x0_ref[rows, cols],
            factor,
            remainder,
            model_width,
        )


def update_kernel(
    model_width, cols, own_ref, peer_ref, x0_ref, weight_ref, remainder_ref, factor_ref, *out_refs
):
    gram = own_ref[...].astype(f32) + peer_ref[...].astype(f32)
    factor, remainder = update_matrix(gram)
    remainder_ref[...] = remainder
    factor_ref[...] = jnp.broadcast_to(factor, factor_ref.shape)
    renew_pieces(model_width, cols, x0_ref, weight_ref, factor, remainder[:, cols], out_refs)


def later_kernel(model_width, cols, remainder_ref, factor_ref, x0_ref, weight_ref, *out_refs):
    remainder = remainder_ref[:, cols]
    renew_pieces(model_width, cols, x0_ref, weight_ref, factor_ref[:1, :1], remainder, out_refs)


def choose_kernel(
    hosts, old_ref, new_ref, own_ref, peer_ref, ids_ref, peer_ids_ref, which_ref, *out_refs
):
    _, rows, chunk = out_refs[0].shape
    group, plane, half = own_place()
    planes = old_ref.shape[1]
    for k in range(len(out_refs)):
        for rel in range(2):
            wanted_slot = 2 * plane + (half ^ rel)
            owner = lax.div(wanted_slot, hosts)
            expert = new_ref[group ^ k, wanted_slot]
            holder = jnp.int32(0)
            for p in range(planes):
                holder = jnp.where(old_ref[owner, p] == expert, p, holder)
            which_ref[2 * k + rel] = plane ^ holder
    for rel, (ref, ids) in enumerate(((own_ref, ids_ref), (peer_ref, peer_ids_ref))):
        place = lax.broadcasted_iota(jnp.int32, (rows, rows), 0)
        pick = jnp.where(place == ids[...], 1.0, 0.0).astype(bf16)
        for k, out in enumerate(out_refs):
            count = chunk // LANES
            cols = half_columns(ref, (group ^ k) * count, count, half)
            out[rel] = tdot(pick, cols).astype(bf16)


def route_kernel(count, *refs):
    ins, outs, store = refs[:count], refs[count : 2 * count], refs[2 * count]
    group, plane, _ = own_place()
    for k in range(count):
        store[k] = ins[k][...]
    for k in range(count):
        outs[k][...] = store[group ^ plane ^ k]


def project_kernel(count, planes, stages, which_ref, *refs):
    toks, weights = refs[:count], refs[count : count + planes * stages]
    keep_ref, send_ref = refs[count + planes * stages :][:2]
    stores = refs[count + planes * stages + 2 :]
    for stage in range(stages):
        for k in range(planes):
            stores[stage][k] = weights[stage * planes + k][...]
    for rel in (1, 0):
        for k in range(count):
            place = which_ref[2 * k + rel]
            start = 0
            for store in stores:
                cols = slice(start, start + store.shape[2])
                start = cols.stop
                got = jnp.dot(toks[k][rel], store[place], preferred_element_type=f32)
                if rel == 0:
                    keep_ref[k, :, cols] = got
                else:
                    send_ref[k, :, cols] = got.astype(bf16)


def join_kernel(count, keep_ref, other_ref, *out_refs):
    for k in range(count):
        out_refs[k][...] = (keep_ref[k] + other_ref[k].astype(f32)).astype(bf16)


def finish_kernel(count, *refs):
    out_ref = refs[-1]
    start = 0
    for tail in range(len(TAILS)):
        mine = refs[tail * count : (tail + 1) * count]
        cols = slice(start, start + mine[0].shape[1])
        start = cols.stop
        out_ref[:, cols] = sum(r[...].astype(f32) for r in mine).astype(out_ref.dtype)


VMEM, SMEM, HBM = pltpu.VMEM, pltpu.SMEM, pltpu.HBM


def call(kernel, arrays, outs, scratch=(), spaces=None, out_spaces=None):
    spaces = spaces or [VMEM] * len(arrays)
    out_spaces = out_spaces or [VMEM] * len(outs)
    made = {
        VMEM: lambda shape, dtype: pltpu.VMEM(shape, dtype),
        SMEM: lambda shape, dtype: pltpu.SMEM(shape, dtype),
        None: jax.ShapeDtypeStruct,
    }
    return pl.pallas_call(
        kernel,
        out_shape=[made[where](*out) for where, out in zip(out_spaces, outs)],
        in_specs=[pl.BlockSpec(memory_space=where or SMEM) for where in spaces],
        out_specs=[pl.BlockSpec(memory_space=where or VMEM) for where in out_spaces],
        scratch_shapes=list(scratch),
        compiler_params=pltpu.CompilerParams(vmem_limit_bytes=16 * 2**20),
    )(
        *[
            a if where is None else pltpu.with_memory_space_constraint(a, where)
            for where, a in zip(spaces, arrays)
        ]
    )


def on_device(tokens, cotangent, weight_halves, momentum_halves, old_map, new_map, row_ids):
    slot_count = lax.axis_size("slot")
    group_count = lax.axis_size("group")
    planes = slot_count // 2
    inputs = (
        tokens,
        cotangent,
        weight_halves[0],
        momentum_halves[0],
        old_map,
        new_map,
        row_ids,
    )
    fits = group_count == planes and planes <= MOST_PERMUTES
    if fits and tokens.shape[1] == 2 * slot_count * LANES:
        return by_permutes(*inputs)
    return by_all_to_all(*inputs)


FIRST = (3, 1, 2)
ACROSS = (3, 2, 1)


def spread(mine, axis, stride, order):
    landed = [mine[0]] + [None] * (len(mine) - 1)
    for k in order:
        if k < len(mine):
            landed[k] = shifted(mine[k], axis, stride, k)
    return landed


def by_permutes(tokens, cotangent, weight, momentum, old_map, new_map, row_ids):
    slot_count = lax.axis_size("slot")
    count = lax.axis_size("group")
    planes = slot_count // 2
    hosts = slot_count // count
    row_count, model_width = tokens.shape
    hidden = cotangent.shape[1]
    half_rows = model_width // 2
    chunk = half_rows // count
    columns = stage_columns(hidden)

    peer_tokens = swapped(tokens)
    peer_cot = swapped(cotangent)

    def loaded(*arrays):
        return call(
            functools.partial(load_kernel, len(arrays)),
            arrays,
            [(a.shape, a.dtype) for a in arrays],
            [pltpu.SemaphoreType.DMA((len(arrays),))],
            spaces=[HBM] * len(arrays),
        )

    tokens_in, cot_in, momentum_in = loaded(tokens, cotangent, momentum)
    x0, own_gram = call(
        front_kernel,
        [tokens_in, peer_tokens, cot_in, peer_cot, momentum_in],
        [((half_rows, hidden), bf16), ((hidden, hidden), bf16)],
    )
    peer_gram = swapped(own_gram)
    weight_in, ids_in = loaded(weight, row_ids)
    peer_ids = swapped(row_ids)

    which, *token_cuts = call(
        functools.partial(choose_kernel, hosts),
        [old_map, new_map, tokens_in, peer_tokens, ids_in, peer_ids],
        [((2 * count,), jnp.int32)] + [((2, row_count, chunk), bf16)] * count,
        spaces=[None, None] + [VMEM] * 4,
        out_spaces=[SMEM] + [VMEM] * count,
    )

    arrived = []
    for stage, cols in enumerate(columns):
        width = cols.stop - cols.start
        if stage == 0:
            remainder, factor, *pieces = call(
                functools.partial(update_kernel, model_width, cols),
                [own_gram, peer_gram, x0, weight_in],
                [((hidden, hidden), bf16), ((8, LANES), f32)] + [((chunk, width), bf16)] * count,
            )
        else:
            pieces = call(
                functools.partial(later_kernel, model_width, cols),
                [remainder, factor, x0, weight_in],
                [((chunk, width), bf16)] * count,
            )
        landed = spread(pieces, "group", 1, FIRST)
        routed = call(
            functools.partial(route_kernel, count),
            landed,
            [((chunk, width), bf16)] * count,
            [pltpu.VMEM((count, chunk, width), bf16)],
        )
        arrived.append(spread(routed, "slot", 2, ACROSS))

    requested = spread(token_cuts, "group", 1, FIRST)

    returned = []
    for stages in TAILS:
        widths = [columns[i].stop - columns[i].start for i in stages]
        keep, send = call(
            functools.partial(project_kernel, count, planes, len(stages)),
            [which] + requested + sum((arrived[i] for i in stages), []),
            [((count, row_count, sum(widths)), f32), ((count, row_count, sum(widths)), bf16)],
            [pltpu.VMEM((planes, chunk, width), bf16) for width in widths],
            spaces=[SMEM] + [VMEM] * (count + planes * len(stages)),
        )
        other = swapped(send)
        mine = call(
            functools.partial(join_kernel, count),
            [keep, other],
            [((row_count, sum(widths)), bf16)] * count,
        )
        returned += spread(mine, "group", 1, FIRST)
    return call(
        functools.partial(finish_kernel, count),
        returned,
        [((row_count, hidden), bf16)],
        out_spaces=[None],
    )[0]


def by_all_to_all(tokens, cotangent, weight, momentum, old_map, new_map, row_ids):
    slot_count = lax.axis_size("slot")
    group_count = lax.axis_size("group")
    planes = slot_count // 2
    owners = max(1, 2 * group_count // slot_count)
    row_count, model_width = tokens.shape
    hidden = cotangent.shape[1]
    half_rows = model_width // 2
    chunk = half_rows // group_count
    half = lax.axis_index("slot") % 2
    plane = lax.axis_index("slot") // 2
    group = lax.axis_index("group")
    hosts = slot_count // group_count

    from_group = group ^ jnp.arange(group_count)
    wanted_slot = 2 * plane + (half ^ jnp.arange(2))
    experts = new_map[from_group[:, None], wanted_slot[None, :]]
    lists = old_map[wanted_slot // hosts]
    holder = jnp.argmax((lists[None] == experts[:, :, None]).astype(jnp.int32), axis=2)

    peer_cot = swapped(cotangent)
    peer_tokens = swapped(pick_columns(tokens, 1 - half, slot_count))
    own_tokens = pick_columns(tokens, half, slot_count)
    gradient = tdot(own_tokens, cotangent) + tdot(peer_tokens, peer_cot)
    x0 = (momentum_rate * momentum.astype(f32) + gradient).astype(bf16)
    own_gram = tdot(x0, x0).astype(bf16)
    factor, remainder = update_matrix(own_gram.astype(f32) + swapped(own_gram).astype(f32))
    renewed = renew(weight, x0, x0, factor, remainder, model_width)

    pick = (row_ids[0][:, None] == jnp.arange(row_count)[None, :]).astype(bf16)
    chosen = jnp.dot(pick, tokens, preferred_element_type=f32).astype(bf16)
    own_chosen = pick_columns(chosen, half, slot_count)
    peer_chosen = swapped(pick_columns(chosen, 1 - half, slot_count))
    both = jnp.stack([own_chosen, peer_chosen]).reshape(2, row_count, group_count, chunk)
    requested = jnp.stack(exchange(lambda d: both[:, :, d], "group", 1))
    outputs = []
    for cols in (slice(0, hidden // 2), slice(hidden // 2, hidden)):
        width = cols.stop - cols.start
        chunks = renewed[:, cols].reshape(group_count, chunk, width)
        in_plane = jnp.stack(exchange(lambda d: chunks[d], "group", 1))
        by_owner = jnp.take(in_plane, group ^ jnp.arange(group_count), axis=0)
        by_plane = by_owner.reshape(planes, owners, chunk, width)
        arrived = jnp.stack(exchange(lambda d: by_plane[d], "slot", 2))
        partial = [
            jnp.einsum(
                "ktc,kcw->ktw",
                requested[:, rel],
                arrived[plane ^ holder[:, rel], (half ^ rel) * owners // 2],
                preferred_element_type=f32,
            )
            for rel in range(2)
        ]
        other = swapped(partial[1].astype(bf16))
        summed = (partial[0] + other.astype(f32)).astype(bf16)
        by_group = jnp.take(summed, group ^ jnp.arange(group_count), axis=0)
        returned = exchange(lambda d: by_group[d], "group", 1)
        outputs.append(sum(r.astype(f32) for r in returned).astype(bf16))
    return jnp.concatenate(outputs, axis=1)


def solution(mesh):
    placed = (
        P(("group", "slot"), None),
        P(("group", "slot"), None),
        P(("group", "slot"), None, None),
        P(("group", "slot"), None, None),
        P(),
        P(),
        P(("group", "slot"), None),
    )
    return jax.shard_map(
        on_device, mesh=mesh, in_specs=placed, out_specs=P(("group", "slot"), None), check_vma=False
    )
```

```python
import functools
import math

import jax
import jax.numpy as jnp
from jax import lax
from jax.experimental import pallas as pl
from jax.experimental.pallas import tpu as pltpu
from jax.sharding import PartitionSpec as P


coef_a = 3.4445
coef_b = -4.775
coef_c = 2.0315
momentum_rate = 0.95
step_scale = 0.01
gram_eps = 1e-06
contract_rows = (((0,), (0,)), ((), ()))
WIDTHS = (1, 1)
TAILS = ((0,), (1,))
MOST_PERMUTES = 4
LANES = 128
bf16 = jnp.bfloat16
f32 = jnp.float32


def shifted(shard, axis, stride, k):
    size = lax.axis_size(axis)
    return lax.ppermute(shard, axis, [(i, i ^ (k * stride)) for i in range(size)])


def swapped(shard):
    return shifted(shard, "slot", 1, 1)


def exchange(piece, axis, stride):
    size = lax.axis_size(axis)
    count = size // stride
    place = lax.axis_index(axis) // stride
    stacked = jnp.stack([piece(d) for d in range(count)])
    groups = [[first + stride * d for d in range(count)] for first in range(stride)]
    landed = lax.all_to_all(
        stacked,
        axis,
        split_axis=0,
        concat_axis=0,
        tiled=True,
        axis_index_groups=groups if stride > 1 else None,
    )
    return [lax.dynamic_index_in_dim(landed, place ^ k, 0, keepdims=False) for k in range(count)]


def pick_columns(token_block, which_half, slot_count):
    row_count, col_count = token_block.shape
    pieces_view = token_block.reshape(row_count, slot_count, 2, col_count // (2 * slot_count))
    chosen = lax.dynamic_index_in_dim(pieces_view, which_half, axis=2, keepdims=False)
    return chosen.reshape(row_count, col_count // 2)


def matmul(left, right):
    return jnp.dot(left.astype(bf16), right.astype(bf16), preferred_element_type=f32)


def tdot(left, right):
    return lax.dot_general(left, right, contract_rows, preferred_element_type=f32)


def update_matrix(gram):
    on_diagonal = lax.broadcasted_iota(jnp.int32, gram.shape, 0) == lax.broadcasted_iota(
        jnp.int32, gram.shape, 1
    )
    norm_sq = jnp.sum(jnp.where(on_diagonal, gram, 0.0), keepdims=True) + gram_eps
    first = gram * (1.0 / norm_sq)
    poly_first = coef_b * first + coef_c * matmul(first, first)
    half_way = coef_a * first + matmul(first, poly_first)
    second = coef_a * half_way + matmul(poly_first, half_way)
    poly_second = coef_b * second + coef_c * matmul(second, second)
    remainder = coef_a * (poly_first + poly_second) + matmul(poly_first, poly_second)
    return lax.rsqrt(norm_sq), remainder.astype(bf16)


def renew(weight, x0, x0_cols, factor, remainder, model_width):
    moved = coef_a * coef_a * x0_cols.astype(f32) + matmul(x0, remainder)
    scale = step_scale * math.sqrt(model_width) * factor
    return (weight.astype(f32) - scale * moved).astype(bf16)


def load_kernel(count, *refs):
    sources, targets, sems = refs[:count], refs[count : 2 * count], refs[2 * count]
    copies = [pltpu.make_async_copy(sources[i], targets[i], sems.at[i]) for i in range(count)]
    for copy in copies:
        copy.start()
    for copy in copies:
        copy.wait()


def own_place():
    slot = lax.axis_index("slot")
    return lax.axis_index("group"), lax.div(slot, 2), lax.rem(slot, 2)


def half_columns(ref, first, count, half):
    parts = []
    for j in range(count):
        start = (2 * (first + j) + half) * LANES
        parts.append(ref[:, pl.ds(pl.multiple_of(start, LANES), LANES)])
    return jnp.concatenate(parts, axis=1)


def front_kernel(own_ref, peer_ref, cot_ref, peer_cot_ref, momentum_ref, x0_ref, gram_ref):
    rows = x0_ref.shape[0]
    half = own_place()[2]
    cots = jnp.concatenate([cot_ref[...], peer_cot_ref[...]], axis=0)
    gram = None
    block = 2 * LANES
    for i in range(rows // block):
        toks = jnp.concatenate(
            [half_columns(ref, 2 * i, 2, half) for ref in (own_ref, peer_ref)], axis=0
        )
        part = slice(i * block, (i + 1) * block)
        x0 = momentum_rate * momentum_ref[part].astype(f32) + tdot(toks, cots)
        x0 = x0.astype(bf16)
        x0_ref[part] = x0
        middle = x0.shape[1] // 2
        left, right = x0[:, :middle], x0[:, middle:]
        term = (tdot(left, x0), tdot(right, right))
        gram = term if gram is None else (gram[0] + term[0], gram[1] + term[1])
    gram_ref[...] = jnp.concatenate(gram, axis=1).astype(bf16)


def stage_columns(hidden):
    unit = hidden // sum(WIDTHS)
    starts = [unit * sum(WIDTHS[:i]) for i in range(len(WIDTHS))]
    return [slice(start, start + unit * share) for start, share in zip(starts, WIDTHS)]


def renew_pieces(model_width, cols, x0_ref, weight_ref, factor, remainder, out_refs):
    group = own_place()[0]
    chunk = out_refs[0].shape[0]
    for k in range(len(out_refs)):
        rows = pl.ds(pl.multiple_of((group ^ k) * chunk, chunk), chunk)
        out_refs[k][...] = renew(
            weight_ref[rows, cols],
            x0_ref[rows, :],
            x0_ref[rows, cols],
            factor,
            remainder,
            model_width,
        )


def update_kernel(
    model_width,
    cols,
    own_ref,
    peer_ref,
    x0_ref,
    weight_ref,
    remainder_ref,
    factor_ref,
    *refs,
):
    out_refs, scratch = refs[:-7], refs[-7:]
    gram_bf, poly_bf, half_bf, second_bf, poly_ref, half_ref, second_ref = scratch
    hidden = gram_bf.shape[0]
    middle = hidden // 2
    upper = own_ref[...].astype(f32) + peer_ref[...].astype(f32)
    corners = upper[:, :middle] + upper[:, hidden:]
    on_diagonal = lax.broadcasted_iota(jnp.int32, corners.shape, 0) == lax.broadcasted_iota(
        jnp.int32, corners.shape, 1
    )
    norm_sq = jnp.sum(jnp.where(on_diagonal, corners, 0.0), keepdims=True) + gram_eps
    inverse = 1.0 / norm_sq
    lower = jnp.concatenate([upper[:, middle:hidden].T, upper[:, hidden:]], axis=1)
    grams = (upper[:, :hidden], lower)
    blocks = (slice(0, middle), slice(middle, hidden))
    for part, gram in zip(blocks, grams):
        gram_bf[part] = gram.astype(bf16)
    for part, gram in zip(blocks, grams):
        first = gram * inverse
        square = jnp.dot(gram_bf[part], gram_bf[...], preferred_element_type=f32)
        poly = coef_b * first + (coef_c * inverse * inverse) * square
        poly_ref[part] = poly
        poly_bf[part] = poly.astype(bf16)
        half = coef_a * first + inverse * jnp.dot(
            poly_bf[part], gram_bf[...], preferred_element_type=f32
        )
        half_ref[part] = half
        half_bf[part] = half.astype(bf16)
    for part in blocks:
        second = coef_a * half_ref[part] + jnp.dot(
            half_bf[part], poly_bf[...], preferred_element_type=f32
        )
        second_ref[part] = second
        second_bf[part] = second.astype(bf16)
    for part in blocks:
        square = jnp.dot(second_bf[part], second_bf[...], preferred_element_type=f32)
        poly = coef_b * second_ref[part] + coef_c * square
        crossed = jnp.dot(poly.astype(bf16), poly_bf[...], preferred_element_type=f32)
        remainder_ref[part] = (coef_a * (poly_ref[part] + poly) + crossed).astype(bf16)
    factor = lax.rsqrt(norm_sq)
    factor_ref[...] = jnp.broadcast_to(factor, factor_ref.shape)
    remainder = remainder_ref[:, cols]
    renew_pieces(model_width, cols, x0_ref, weight_ref, factor, remainder, out_refs)


def later_kernel(model_width, cols, remainder_ref, factor_ref, x0_ref, weight_ref, *out_refs):
    remainder = remainder_ref[:, cols]
    renew_pieces(model_width, cols, x0_ref, weight_ref, factor_ref[:1, :1], remainder, out_refs)


def choose_kernel(
    hosts, old_ref, new_ref, own_ref, peer_ref, ids_ref, peer_ids_ref, which_ref, *out_refs
):
    _, rows, chunk = out_refs[0].shape
    group, plane, half = own_place()
    planes = old_ref.shape[1]
    for k in range(len(out_refs)):
        for rel in range(2):
            wanted_slot = 2 * plane + (half ^ rel)
            owner = lax.div(wanted_slot, hosts)
            expert = new_ref[group ^ k, wanted_slot]
            holder = jnp.int32(0)
            for p in range(planes):
                holder = jnp.where(old_ref[owner, p] == expert, p, holder)
            which_ref[2 * k + rel] = plane ^ holder
    for rel, (ref, ids) in enumerate(((own_ref, ids_ref), (peer_ref, peer_ids_ref))):
        place = lax.broadcasted_iota(jnp.int32, (rows, rows), 0)
        pick = jnp.where(place == ids[...], 1.0, 0.0).astype(bf16)
        for k, out in enumerate(out_refs):
            count = chunk // LANES
            cols = half_columns(ref, (group ^ k) * count, count, half)
            out[rel] = tdot(pick, cols).astype(bf16)


def route_kernel(count, *refs):
    ins, outs, store = refs[:count], refs[count : 2 * count], refs[2 * count]
    group, plane, _ = own_place()
    for k in range(count):
        store[k] = ins[k][...]
    for k in range(count):
        outs[k][...] = store[group ^ plane ^ k]


def project_kernel(count, planes, stages, which_ref, *refs):
    toks, weights = refs[:count], refs[count : count + planes * stages]
    keep_ref, send_ref = refs[count + planes * stages :][:2]
    stores = refs[count + planes * stages + 2 :]
    for stage in range(stages):
        for k in range(planes):
            stores[stage][k] = weights[stage * planes + k][...]
    for rel in (1, 0):
        for k in range(count):
            place = which_ref[2 * k + rel]
            start = 0
            for store in stores:
                cols = slice(start, start + store.shape[2])
                start = cols.stop
                got = jnp.dot(toks[k][rel], store[place], preferred_element_type=f32)
                if rel == 0:
                    keep_ref[k, :, cols] = got
                else:
                    send_ref[k, :, cols] = got.astype(bf16)


def join_kernel(count, keep_ref, other_ref, *out_refs):
    for k in range(count):
        out_refs[k][...] = (keep_ref[k] + other_ref[k].astype(f32)).astype(bf16)


def finish_kernel(count, *refs):
    out_ref = refs[-1]
    start = 0
    for tail in range(len(TAILS)):
        mine = refs[tail * count : (tail + 1) * count]
        cols = slice(start, start + mine[0].shape[1])
        start = cols.stop
        out_ref[:, cols] = sum(r[...].astype(f32) for r in mine).astype(out_ref.dtype)


VMEM, SMEM, HBM = pltpu.VMEM, pltpu.SMEM, pltpu.HBM


def call(kernel, arrays, outs, scratch=(), spaces=None, out_spaces=None):
    spaces = spaces or [VMEM] * len(arrays)
    out_spaces = out_spaces or [VMEM] * len(outs)
    made = {
        VMEM: lambda shape, dtype: pltpu.VMEM(shape, dtype),
        SMEM: lambda shape, dtype: pltpu.SMEM(shape, dtype),
        None: jax.ShapeDtypeStruct,
    }
    return pl.pallas_call(
        kernel,
        out_shape=[made[where](*out) for where, out in zip(out_spaces, outs)],
        in_specs=[pl.BlockSpec(memory_space=where or SMEM) for where in spaces],
        out_specs=[pl.BlockSpec(memory_space=where or VMEM) for where in out_spaces],
        scratch_shapes=list(scratch),
        compiler_params=pltpu.CompilerParams(vmem_limit_bytes=16 * 2**20),
    )(
        *[
            a if where is None else pltpu.with_memory_space_constraint(a, where)
            for where, a in zip(spaces, arrays)
        ]
    )


def on_device(tokens, cotangent, weight_halves, momentum_halves, old_map, new_map, row_ids):
    slot_count = lax.axis_size("slot")
    group_count = lax.axis_size("group")
    planes = slot_count // 2
    inputs = (
        tokens,
        cotangent,
        weight_halves[0],
        momentum_halves[0],
        old_map,
        new_map,
        row_ids,
    )
    fits = group_count == planes and planes <= MOST_PERMUTES
    if fits and tokens.shape[1] == 2 * slot_count * LANES:
        return by_permutes(*inputs)
    return by_all_to_all(*inputs)


FIRST = (3, 2, 1)
ACROSS = (3, 2, 1)


def spread(mine, axis, stride, order):
    landed = [mine[0]] + [None] * (len(mine) - 1)
    for k in order:
        if k < len(mine):
            landed[k] = shifted(mine[k], axis, stride, k)
    return landed


def by_permutes(tokens, cotangent, weight, momentum, old_map, new_map, row_ids):
    slot_count = lax.axis_size("slot")
    count = lax.axis_size("group")
    planes = slot_count // 2
    hosts = slot_count // count
    row_count, model_width = tokens.shape
    hidden = cotangent.shape[1]
    half_rows = model_width // 2
    chunk = half_rows // count
    columns = stage_columns(hidden)

    peer_tokens = swapped(tokens)
    peer_cot = swapped(cotangent)

    def loaded(*arrays):
        return call(
            functools.partial(load_kernel, len(arrays)),
            arrays,
            [(a.shape, a.dtype) for a in arrays],
            [pltpu.SemaphoreType.DMA((len(arrays),))],
            spaces=[HBM] * len(arrays),
        )

    tokens_in, cot_in, momentum_in = loaded(tokens, cotangent, momentum)
    x0, own_gram = call(
        front_kernel,
        [tokens_in, peer_tokens, cot_in, peer_cot, momentum_in],
        [((half_rows, hidden), bf16), ((hidden // 2, hidden + hidden // 2), bf16)],
    )
    peer_gram = swapped(own_gram)
    weight_in, ids_in = loaded(weight, row_ids)
    peer_ids = swapped(row_ids)

    which, *token_cuts = call(
        functools.partial(choose_kernel, hosts),
        [old_map, new_map, tokens_in, peer_tokens, ids_in, peer_ids],
        [((2 * count,), jnp.int32)] + [((2, row_count, chunk), bf16)] * count,
        spaces=[None, None] + [VMEM] * 4,
        out_spaces=[SMEM] + [VMEM] * count,
    )

    arrived = []
    for stage, cols in enumerate(columns):
        width = cols.stop - cols.start
        if stage == 0:
            remainder, factor, *pieces = call(
                functools.partial(update_kernel, model_width, cols),
                [own_gram, peer_gram, x0, weight_in],
                [((hidden, hidden), bf16), ((8, LANES), f32)] + [((chunk, width), bf16)] * count,
                [pltpu.VMEM((hidden, hidden), bf16)] * 4
                + [pltpu.VMEM((hidden, hidden), f32)] * 3,
            )
        else:
            pieces = call(
                functools.partial(later_kernel, model_width, cols),
                [remainder, factor, x0, weight_in],
                [((chunk, width), bf16)] * count,
            )
        landed = spread(pieces, "group", 1, FIRST)
        routed = call(
            functools.partial(route_kernel, count),
            landed,
            [((chunk, width), bf16)] * count,
            [pltpu.VMEM((count, chunk, width), bf16)],
        )
        arrived.append(spread(routed, "slot", 2, ACROSS))

    requested = spread(token_cuts, "group", 1, FIRST)

    returned = []
    for stages in TAILS:
        widths = [columns[i].stop - columns[i].start for i in stages]
        keep, send = call(
            functools.partial(project_kernel, count, planes, len(stages)),
            [which] + requested + sum((arrived[i] for i in stages), []),
            [((count, row_count, sum(widths)), f32), ((count, row_count, sum(widths)), bf16)],
            [pltpu.VMEM((planes, chunk, width), bf16) for width in widths],
            spaces=[SMEM] + [VMEM] * (count + planes * len(stages)),
        )
        other = swapped(send)
        mine = call(
            functools.partial(join_kernel, count),
            [keep, other],
            [((row_count, sum(widths)), bf16)] * count,
        )
        returned += spread(mine, "group", 1, FIRST)
    return call(
        functools.partial(finish_kernel, count),
        returned,
        [((row_count, hidden), bf16)],
        out_spaces=[None],
    )[0]


def by_all_to_all(tokens, cotangent, weight, momentum, old_map, new_map, row_ids):
    slot_count = lax.axis_size("slot")
    group_count = lax.axis_size("group")
    planes = slot_count // 2
    owners = max(1, 2 * group_count // slot_count)
    row_count, model_width = tokens.shape
    hidden = cotangent.shape[1]
    half_rows = model_width // 2
    chunk = half_rows // group_count
    half = lax.axis_index("slot") % 2
    plane = lax.axis_index("slot") // 2
    group = lax.axis_index("group")
    hosts = slot_count // group_count

    from_group = group ^ jnp.arange(group_count)
    wanted_slot = 2 * plane + (half ^ jnp.arange(2))
    experts = new_map[from_group[:, None], wanted_slot[None, :]]
    lists = old_map[wanted_slot // hosts]
    holder = jnp.argmax((lists[None] == experts[:, :, None]).astype(jnp.int32), axis=2)

    peer_cot = swapped(cotangent)
    peer_tokens = swapped(pick_columns(tokens, 1 - half, slot_count))
    own_tokens = pick_columns(tokens, half, slot_count)
    gradient = tdot(own_tokens, cotangent) + tdot(peer_tokens, peer_cot)
    x0 = (momentum_rate * momentum.astype(f32) + gradient).astype(bf16)
    own_gram = tdot(x0, x0).astype(bf16)
    factor, remainder = update_matrix(own_gram.astype(f32) + swapped(own_gram).astype(f32))
    renewed = renew(weight, x0, x0, factor, remainder, model_width)

    pick = (row_ids[0][:, None] == jnp.arange(row_count)[None, :]).astype(bf16)
    chosen = jnp.dot(pick, tokens, preferred_element_type=f32).astype(bf16)
    own_chosen = pick_columns(chosen, half, slot_count)
    peer_chosen = swapped(pick_columns(chosen, 1 - half, slot_count))
    both = jnp.stack([own_chosen, peer_chosen]).reshape(2, row_count, group_count, chunk)
    requested = jnp.stack(exchange(lambda d: both[:, :, d], "group", 1))
    outputs = []
    for cols in (slice(0, hidden // 2), slice(hidden // 2, hidden)):
        width = cols.stop - cols.start
        chunks = renewed[:, cols].reshape(group_count, chunk, width)
        in_plane = jnp.stack(exchange(lambda d: chunks[d], "group", 1))
        by_owner = jnp.take(in_plane, group ^ jnp.arange(group_count), axis=0)
        by_plane = by_owner.reshape(planes, owners, chunk, width)
        arrived = jnp.stack(exchange(lambda d: by_plane[d], "slot", 2))
        partial = [
            jnp.einsum(
                "ktc,kcw->ktw",
                requested[:, rel],
                arrived[plane ^ holder[:, rel], (half ^ rel) * owners // 2],
                preferred_element_type=f32,
            )
            for rel in range(2)
        ]
        other = swapped(partial[1].astype(bf16))
        summed = (partial[0] + other.astype(f32)).astype(bf16)
        by_group = jnp.take(summed, group ^ jnp.arange(group_count), axis=0)
        returned = exchange(lambda d: by_group[d], "group", 1)
        outputs.append(sum(r.astype(f32) for r in returned).astype(bf16))
    return jnp.concatenate(outputs, axis=1)


def solution(mesh):
    placed = (
        P(("group", "slot"), None),
        P(("group", "slot"), None),
        P(("group", "slot"), None, None),
        P(("group", "slot"), None, None),
        P(),
        P(),
        P(("group", "slot"), None),
    )
    return jax.shard_map(
        on_device, mesh=mesh, in_specs=placed, out_specs=P(("group", "slot"), None), check_vma=False
    )
```

```python
import functools
import math

import jax
import jax.numpy as jnp
from jax import lax
from jax.experimental import pallas as pl
from jax.experimental.pallas import tpu as pltpu
from jax.sharding import PartitionSpec as P


coef_a = 3.4445
coef_b = -4.775
coef_c = 2.0315
momentum_rate = 0.95
step_scale = 0.01
gram_eps = 1e-06
contract_rows = (((0,), (0,)), ((), ()))
WIDTHS = (1, 1)
TAILS = ((0,), (1,))
MOST_PERMUTES = 4
LANES = 128
bf16 = jnp.bfloat16
f32 = jnp.float32


def shifted(shard, axis, stride, k):
    size = lax.axis_size(axis)
    return lax.ppermute(shard, axis, [(i, i ^ (k * stride)) for i in range(size)])


def swapped(shard):
    return shifted(shard, "slot", 1, 1)


def exchange(piece, axis, stride):
    size = lax.axis_size(axis)
    count = size // stride
    place = lax.axis_index(axis) // stride
    stacked = jnp.stack([piece(d) for d in range(count)])
    groups = [[first + stride * d for d in range(count)] for first in range(stride)]
    landed = lax.all_to_all(
        stacked,
        axis,
        split_axis=0,
        concat_axis=0,
        tiled=True,
        axis_index_groups=groups if stride > 1 else None,
    )
    return [lax.dynamic_index_in_dim(landed, place ^ k, 0, keepdims=False) for k in range(count)]


def pick_columns(token_block, which_half, slot_count):
    row_count, col_count = token_block.shape
    pieces_view = token_block.reshape(row_count, slot_count, 2, col_count // (2 * slot_count))
    chosen = lax.dynamic_index_in_dim(pieces_view, which_half, axis=2, keepdims=False)
    return chosen.reshape(row_count, col_count // 2)


def matmul(left, right):
    return jnp.dot(left.astype(bf16), right.astype(bf16), preferred_element_type=f32)


def tdot(left, right):
    return lax.dot_general(left, right, contract_rows, preferred_element_type=f32)


def update_matrix(gram):
    on_diagonal = lax.broadcasted_iota(jnp.int32, gram.shape, 0) == lax.broadcasted_iota(
        jnp.int32, gram.shape, 1
    )
    norm_sq = jnp.sum(jnp.where(on_diagonal, gram, 0.0), keepdims=True) + gram_eps
    first = gram * (1.0 / norm_sq)
    poly_first = coef_b * first + coef_c * matmul(first, first)
    half_way = coef_a * first + matmul(first, poly_first)
    second = coef_a * half_way + matmul(poly_first, half_way)
    poly_second = coef_b * second + coef_c * matmul(second, second)
    remainder = coef_a * (poly_first + poly_second) + matmul(poly_first, poly_second)
    return lax.rsqrt(norm_sq), remainder.astype(bf16)


def renew(weight, x0, x0_cols, factor, remainder, model_width):
    moved = coef_a * coef_a * x0_cols.astype(f32) + matmul(x0, remainder)
    scale = step_scale * math.sqrt(model_width) * factor
    return (weight.astype(f32) - scale * moved).astype(bf16)


def load_kernel(count, *refs):
    sources, targets, sems = refs[:count], refs[count : 2 * count], refs[2 * count]
    copies = [pltpu.make_async_copy(sources[i], targets[i], sems.at[i]) for i in range(count)]
    for copy in copies:
        copy.start()
    for copy in copies:
        copy.wait()


def own_place():
    slot = lax.axis_index("slot")
    return lax.axis_index("group"), lax.div(slot, 2), lax.rem(slot, 2)


def half_columns(ref, first, count, half):
    parts = []
    for j in range(count):
        start = (2 * (first + j) + half) * LANES
        parts.append(ref[:, pl.ds(pl.multiple_of(start, LANES), LANES)])
    return jnp.concatenate(parts, axis=1)


def front_kernel(own_ref, peer_ref, cot_ref, peer_cot_ref, momentum_ref, x0_ref, gram_ref):
    rows = x0_ref.shape[0]
    half = own_place()[2]
    cots = jnp.concatenate([cot_ref[...], peer_cot_ref[...]], axis=0)
    gram = None
    block = 2 * LANES
    for i in range(rows // block):
        toks = jnp.concatenate(
            [half_columns(ref, 2 * i, 2, half) for ref in (own_ref, peer_ref)], axis=0
        )
        part = slice(i * block, (i + 1) * block)
        x0 = momentum_rate * momentum_ref[part].astype(f32) + tdot(toks, cots)
        x0 = x0.astype(bf16)
        x0_ref[part] = x0
        middle = x0.shape[1] // 2
        left, right = x0[:, :middle], x0[:, middle:]
        term = (tdot(left, x0), tdot(right, right))
        gram = term if gram is None else (gram[0] + term[0], gram[1] + term[1])
    gram_ref[...] = jnp.concatenate(gram, axis=1).astype(bf16)


def stage_columns(hidden):
    unit = hidden // sum(WIDTHS)
    starts = [unit * sum(WIDTHS[:i]) for i in range(len(WIDTHS))]
    return [slice(start, start + unit * share) for start, share in zip(starts, WIDTHS)]


def renew_pieces(model_width, cols, which, x0_ref, weight_ref, factor, remainder, out_refs):
    group = own_place()[0]
    chunk = out_refs[0].shape[0]
    for k, out_ref in zip(which, out_refs):
        rows = pl.ds(pl.multiple_of((group ^ k) * chunk, chunk), chunk)
        out_ref[...] = renew(
            weight_ref[rows, cols],
            x0_ref[rows, :],
            x0_ref[rows, cols],
            factor,
            remainder,
            model_width,
        )


def update_kernel(
    model_width,
    cols,
    which,
    own_ref,
    peer_ref,
    x0_ref,
    weight_ref,
    remainder_ref,
    factor_ref,
    *refs,
):
    out_refs, scratch = refs[:-7], refs[-7:]
    gram_bf, poly_bf, half_bf, second_bf, poly_ref, half_ref, second_ref = scratch
    hidden = gram_bf.shape[0]
    middle = hidden // 2
    upper = own_ref[...].astype(f32) + peer_ref[...].astype(f32)
    corners = upper[:, :middle] + upper[:, hidden:]
    on_diagonal = lax.broadcasted_iota(jnp.int32, corners.shape, 0) == lax.broadcasted_iota(
        jnp.int32, corners.shape, 1
    )
    norm_sq = jnp.sum(jnp.where(on_diagonal, corners, 0.0), keepdims=True) + gram_eps
    inverse = 1.0 / norm_sq
    lower = jnp.concatenate([upper[:, middle:hidden].T, upper[:, hidden:]], axis=1)
    grams = (upper[:, :hidden], lower)
    blocks = (slice(0, middle), slice(middle, hidden))
    for part, gram in zip(blocks, grams):
        gram_bf[part] = gram.astype(bf16)
    for part, gram in zip(blocks, grams):
        first = gram * inverse
        square = jnp.dot(gram_bf[part], gram_bf[...], preferred_element_type=f32)
        poly = coef_b * first + (coef_c * inverse * inverse) * square
        poly_ref[part] = poly
        poly_bf[part] = poly.astype(bf16)
        half = coef_a * first + inverse * jnp.dot(
            poly_bf[part], gram_bf[...], preferred_element_type=f32
        )
        half_ref[part] = half
        half_bf[part] = half.astype(bf16)
    for part in blocks:
        second = coef_a * half_ref[part] + jnp.dot(
            half_bf[part], poly_bf[...], preferred_element_type=f32
        )
        second_ref[part] = second
        second_bf[part] = second.astype(bf16)
    for part in blocks:
        square = jnp.dot(second_bf[part], second_bf[...], preferred_element_type=f32)
        poly = coef_b * second_ref[part] + coef_c * square
        crossed = jnp.dot(poly.astype(bf16), poly_bf[...], preferred_element_type=f32)
        remainder_ref[part] = (coef_a * (poly_ref[part] + poly) + crossed).astype(bf16)
    factor = lax.rsqrt(norm_sq)
    factor_ref[...] = jnp.broadcast_to(factor, factor_ref.shape)
    remainder = remainder_ref[:, cols]
    renew_pieces(model_width, cols, which, x0_ref, weight_ref, factor, remainder, out_refs)


def later_kernel(model_width, cols, which, remainder_ref, factor_ref, x0_ref, weight_ref, *out_refs):
    remainder = remainder_ref[:, cols]
    factor = factor_ref[:1, :1]
    renew_pieces(model_width, cols, which, x0_ref, weight_ref, factor, remainder, out_refs)


def choose_kernel(
    hosts, old_ref, new_ref, own_ref, peer_ref, ids_ref, peer_ids_ref, which_ref, *out_refs
):
    _, rows, chunk = out_refs[0].shape
    group, plane, half = own_place()
    planes = old_ref.shape[1]
    for k in range(len(out_refs)):
        for rel in range(2):
            wanted_slot = 2 * plane + (half ^ rel)
            owner = lax.div(wanted_slot, hosts)
            expert = new_ref[group ^ k, wanted_slot]
            holder = jnp.int32(0)
            for p in range(planes):
                holder = jnp.where(old_ref[owner, p] == expert, p, holder)
            which_ref[2 * k + rel] = plane ^ holder
    for rel, (ref, ids) in enumerate(((own_ref, ids_ref), (peer_ref, peer_ids_ref))):
        place = lax.broadcasted_iota(jnp.int32, (rows, rows), 0)
        pick = jnp.where(place == ids[...], 1.0, 0.0).astype(bf16)
        for k, out in enumerate(out_refs):
            count = chunk // LANES
            cols = half_columns(ref, (group ^ k) * count, count, half)
            out[rel] = tdot(pick, cols).astype(bf16)


def route_kernel(count, *refs):
    ins, outs, store = refs[:count], refs[count : 2 * count], refs[2 * count]
    group, plane, _ = own_place()
    for k in range(count):
        store[k] = ins[k][...]
    for k in range(count):
        outs[k][...] = store[group ^ plane ^ k]


def project_kernel(count, planes, stages, rel, which_ref, *refs):
    toks, weights = refs[:count], refs[count : count + planes * stages]
    out_ref = refs[count + planes * stages]
    stores = refs[count + planes * stages + 1 :]
    for stage in range(stages):
        for k in range(planes):
            stores[stage][k] = weights[stage * planes + k][...]
    for k in range(count):
        place = which_ref[2 * k + rel]
        start = 0
        for store in stores:
            cols = slice(start, start + store.shape[2])
            start = cols.stop
            got = jnp.dot(toks[k][rel], store[place], preferred_element_type=f32)
            out_ref[k, :, cols] = got.astype(out_ref.dtype)


def join_kernel(count, keep_ref, other_ref, *out_refs):
    for k in range(count):
        out_refs[k][...] = (keep_ref[k] + other_ref[k].astype(f32)).astype(bf16)


def finish_kernel(count, *refs):
    out_ref = refs[-1]
    start = 0
    for tail in range(len(TAILS)):
        mine = refs[tail * count : (tail + 1) * count]
        cols = slice(start, start + mine[0].shape[1])
        start = cols.stop
        out_ref[:, cols] = sum(r[...].astype(f32) for r in mine).astype(out_ref.dtype)


VMEM, SMEM, HBM = pltpu.VMEM, pltpu.SMEM, pltpu.HBM


def call(kernel, arrays, outs, scratch=(), spaces=None, out_spaces=None):
    spaces = spaces or [VMEM] * len(arrays)
    out_spaces = out_spaces or [VMEM] * len(outs)
    made = {
        VMEM: lambda shape, dtype: pltpu.VMEM(shape, dtype),
        SMEM: lambda shape, dtype: pltpu.SMEM(shape, dtype),
        None: jax.ShapeDtypeStruct,
    }
    return pl.pallas_call(
        kernel,
        out_shape=[made[where](*out) for where, out in zip(out_spaces, outs)],
        in_specs=[pl.BlockSpec(memory_space=where or SMEM) for where in spaces],
        out_specs=[pl.BlockSpec(memory_space=where or VMEM) for where in out_spaces],
        scratch_shapes=list(scratch),
        compiler_params=pltpu.CompilerParams(vmem_limit_bytes=16 * 2**20),
    )(
        *[
            a if where is None else pltpu.with_memory_space_constraint(a, where)
            for where, a in zip(spaces, arrays)
        ]
    )


def on_device(tokens, cotangent, weight_halves, momentum_halves, old_map, new_map, row_ids):
    slot_count = lax.axis_size("slot")
    group_count = lax.axis_size("group")
    planes = slot_count // 2
    inputs = (
        tokens,
        cotangent,
        weight_halves[0],
        momentum_halves[0],
        old_map,
        new_map,
        row_ids,
    )
    fits = group_count == planes and planes <= MOST_PERMUTES
    if fits and tokens.shape[1] == 2 * slot_count * LANES:
        return by_permutes(*inputs)
    return by_all_to_all(*inputs)


FIRST = (3, 2, 1)
ACROSS = (3, 2, 1)


def spread(mine, axis, stride, order):
    landed = [mine[0]] + [None] * (len(mine) - 1)
    for k in order:
        if k < len(mine):
            landed[k] = shifted(mine[k], axis, stride, k)
    return landed


def by_permutes(tokens, cotangent, weight, momentum, old_map, new_map, row_ids):
    slot_count = lax.axis_size("slot")
    count = lax.axis_size("group")
    planes = slot_count // 2
    hosts = slot_count // count
    row_count, model_width = tokens.shape
    hidden = cotangent.shape[1]
    half_rows = model_width // 2
    chunk = half_rows // count
    columns = stage_columns(hidden)

    peer_tokens = swapped(tokens)
    peer_cot = swapped(cotangent)

    def loaded(*arrays):
        return call(
            functools.partial(load_kernel, len(arrays)),
            arrays,
            [(a.shape, a.dtype) for a in arrays],
            [pltpu.SemaphoreType.DMA((len(arrays),))],
            spaces=[HBM] * len(arrays),
        )

    tokens_in, cot_in, momentum_in = loaded(tokens, cotangent, momentum)
    x0, own_gram = call(
        front_kernel,
        [tokens_in, peer_tokens, cot_in, peer_cot, momentum_in],
        [((half_rows, hidden), bf16), ((hidden // 2, hidden + hidden // 2), bf16)],
    )
    peer_gram = swapped(own_gram)
    weight_in, ids_in = loaded(weight, row_ids)
    peer_ids = swapped(row_ids)

    which, *token_cuts = call(
        functools.partial(choose_kernel, hosts),
        [old_map, new_map, tokens_in, peer_tokens, ids_in, peer_ids],
        [((2 * count,), jnp.int32)] + [((2, row_count, chunk), bf16)] * count,
        spaces=[None, None] + [VMEM] * 4,
        out_spaces=[SMEM] + [VMEM] * count,
    )

    arrived = []
    for stage, cols in enumerate(columns):
        width = cols.stop - cols.start
        pieces = [None] * count
        behind = [k for k in range(count) if stage or k != FIRST[0]]
        if stage == 0:
            remainder, factor, pieces[FIRST[0]] = call(
                functools.partial(update_kernel, model_width, cols, FIRST[:1]),
                [own_gram, peer_gram, x0, weight_in],
                [((hidden, hidden), bf16), ((8, LANES), f32), ((chunk, width), bf16)],
                [pltpu.VMEM((hidden, hidden), bf16)] * 4
                + [pltpu.VMEM((hidden, hidden), f32)] * 3,
            )
        made = call(
            functools.partial(later_kernel, model_width, cols, behind),
            [remainder, factor, x0, weight_in],
            [((chunk, width), bf16)] * len(behind),
        )
        for k, piece in zip(behind, made):
            pieces[k] = piece
        landed = spread(pieces, "group", 1, FIRST)
        routed = call(
            functools.partial(route_kernel, count),
            landed,
            [((chunk, width), bf16)] * count,
            [pltpu.VMEM((count, chunk, width), bf16)],
        )
        arrived.append(spread(routed, "slot", 2, ACROSS))

    requested = spread(token_cuts, "group", 1, FIRST)

    returned = []
    for stages in TAILS:
        widths = [columns[i].stop - columns[i].start for i in stages]

        def projected(rel, dtype):
            return call(
                functools.partial(project_kernel, count, planes, len(stages), rel),
                [which] + requested + sum((arrived[i] for i in stages), []),
                [((count, row_count, sum(widths)), dtype)],
                [pltpu.VMEM((planes, chunk, width), bf16) for width in widths],
                spaces=[SMEM] + [VMEM] * (count + planes * len(stages)),
            )[0]

        send = projected(1, bf16)
        other = swapped(send)
        keep = projected(0, f32)
        mine = call(
            functools.partial(join_kernel, count),
            [keep, other],
            [((row_count, sum(widths)), bf16)] * count,
        )
        returned += spread(mine, "group", 1, FIRST)
    return call(
        functools.partial(finish_kernel, count),
        returned,
        [((row_count, hidden), bf16)],
        out_spaces=[None],
    )[0]


def by_all_to_all(tokens, cotangent, weight, momentum, old_map, new_map, row_ids):
    slot_count = lax.axis_size("slot")
    group_count = lax.axis_size("group")
    planes = slot_count // 2
    owners = max(1, 2 * group_count // slot_count)
    row_count, model_width = tokens.shape
    hidden = cotangent.shape[1]
    half_rows = model_width // 2
    chunk = half_rows // group_count
    half = lax.axis_index("slot") % 2
    plane = lax.axis_index("slot") // 2
    group = lax.axis_index("group")
    hosts = slot_count // group_count

    from_group = group ^ jnp.arange(group_count)
    wanted_slot = 2 * plane + (half ^ jnp.arange(2))
    experts = new_map[from_group[:, None], wanted_slot[None, :]]
    lists = old_map[wanted_slot // hosts]
    holder = jnp.argmax((lists[None] == experts[:, :, None]).astype(jnp.int32), axis=2)

    peer_cot = swapped(cotangent)
    peer_tokens = swapped(pick_columns(tokens, 1 - half, slot_count))
    own_tokens = pick_columns(tokens, half, slot_count)
    gradient = tdot(own_tokens, cotangent) + tdot(peer_tokens, peer_cot)
    x0 = (momentum_rate * momentum.astype(f32) + gradient).astype(bf16)
    own_gram = tdot(x0, x0).astype(bf16)
    factor, remainder = update_matrix(own_gram.astype(f32) + swapped(own_gram).astype(f32))
    renewed = renew(weight, x0, x0, factor, remainder, model_width)

    pick = (row_ids[0][:, None] == jnp.arange(row_count)[None, :]).astype(bf16)
    chosen = jnp.dot(pick, tokens, preferred_element_type=f32).astype(bf16)
    own_chosen = pick_columns(chosen, half, slot_count)
    peer_chosen = swapped(pick_columns(chosen, 1 - half, slot_count))
    both = jnp.stack([own_chosen, peer_chosen]).reshape(2, row_count, group_count, chunk)
    requested = jnp.stack(exchange(lambda d: both[:, :, d], "group", 1))
    outputs = []
    for cols in (slice(0, hidden // 2), slice(hidden // 2, hidden)):
        width = cols.stop - cols.start
        chunks = renewed[:, cols].reshape(group_count, chunk, width)
        in_plane = jnp.stack(exchange(lambda d: chunks[d], "group", 1))
        by_owner = jnp.take(in_plane, group ^ jnp.arange(group_count), axis=0)
        by_plane = by_owner.reshape(planes, owners, chunk, width)
        arrived = jnp.stack(exchange(lambda d: by_plane[d], "slot", 2))
        partial = [
            jnp.einsum(
                "ktc,kcw->ktw",
                requested[:, rel],
                arrived[plane ^ holder[:, rel], (half ^ rel) * owners // 2],
                preferred_element_type=f32,
            )
            for rel in range(2)
        ]
        other = swapped(partial[1].astype(bf16))
        summed = (partial[0] + other.astype(f32)).astype(bf16)
        by_group = jnp.take(summed, group ^ jnp.arange(group_count), axis=0)
        returned = exchange(lambda d: by_group[d], "group", 1)
        outputs.append(sum(r.astype(f32) for r in returned).astype(bf16))
    return jnp.concatenate(outputs, axis=1)


def solution(mesh):
    placed = (
        P(("group", "slot"), None),
        P(("group", "slot"), None),
        P(("group", "slot"), None, None),
        P(("group", "slot"), None, None),
        P(),
        P(),
        P(("group", "slot"), None),
    )
    return jax.shard_map(
        on_device, mesh=mesh, in_specs=placed, out_specs=P(("group", "slot"), None), check_vma=False
    )
```

```python
import functools
import math

import jax
import jax.numpy as jnp
from jax import lax
from jax.experimental import pallas as pl
from jax.experimental.pallas import tpu as pltpu
from jax.sharding import PartitionSpec as P


coef_a = 3.4445
coef_b = -4.775
coef_c = 2.0315
momentum_rate = 0.95
step_scale = 0.01
gram_eps = 1e-06
contract_rows = (((0,), (0,)), ((), ()))
WIDTHS = (1, 1)
TAILS = ((0,), (1,))
MOST_PERMUTES = 4
LANES = 128
bf16 = jnp.bfloat16
f32 = jnp.float32


def shifted(shard, axis, stride, k):
    size = lax.axis_size(axis)
    return lax.ppermute(shard, axis, [(i, i ^ (k * stride)) for i in range(size)])


def swapped(shard):
    return shifted(shard, "slot", 1, 1)


def exchange(piece, axis, stride):
    size = lax.axis_size(axis)
    count = size // stride
    place = lax.axis_index(axis) // stride
    stacked = jnp.stack([piece(d) for d in range(count)])
    groups = [[first + stride * d for d in range(count)] for first in range(stride)]
    landed = lax.all_to_all(
        stacked,
        axis,
        split_axis=0,
        concat_axis=0,
        tiled=True,
        axis_index_groups=groups if stride > 1 else None,
    )
    return [lax.dynamic_index_in_dim(landed, place ^ k, 0, keepdims=False) for k in range(count)]


def pick_columns(token_block, which_half, slot_count):
    row_count, col_count = token_block.shape
    pieces_view = token_block.reshape(row_count, slot_count, 2, col_count // (2 * slot_count))
    chosen = lax.dynamic_index_in_dim(pieces_view, which_half, axis=2, keepdims=False)
    return chosen.reshape(row_count, col_count // 2)


def matmul(left, right):
    return jnp.dot(left.astype(bf16), right.astype(bf16), preferred_element_type=f32)


def tdot(left, right):
    return lax.dot_general(left, right, contract_rows, preferred_element_type=f32)


def update_matrix(gram):
    on_diagonal = lax.broadcasted_iota(jnp.int32, gram.shape, 0) == lax.broadcasted_iota(
        jnp.int32, gram.shape, 1
    )
    norm_sq = jnp.sum(jnp.where(on_diagonal, gram, 0.0), keepdims=True) + gram_eps
    first = gram * (1.0 / norm_sq)
    poly_first = coef_b * first + coef_c * matmul(first, first)
    half_way = coef_a * first + matmul(first, poly_first)
    second = coef_a * half_way + matmul(poly_first, half_way)
    poly_second = coef_b * second + coef_c * matmul(second, second)
    remainder = coef_a * (poly_first + poly_second) + matmul(poly_first, poly_second)
    return lax.rsqrt(norm_sq), remainder.astype(bf16)


def renew(weight, x0, x0_cols, factor, remainder, model_width):
    moved = coef_a * coef_a * x0_cols.astype(f32) + matmul(x0, remainder)
    scale = step_scale * math.sqrt(model_width) * factor
    return (weight.astype(f32) - scale * moved).astype(bf16)


def load_kernel(count, *refs):
    sources, targets, sems = refs[:count], refs[count : 2 * count], refs[2 * count]
    copies = [pltpu.make_async_copy(sources[i], targets[i], sems.at[i]) for i in range(count)]
    for copy in copies:
        copy.start()
    for copy in copies:
        copy.wait()


def own_place():
    slot = lax.axis_index("slot")
    return lax.axis_index("group"), lax.div(slot, 2), lax.rem(slot, 2)


def half_columns(ref, first, count, half):
    parts = []
    for j in range(count):
        start = (2 * (first + j) + half) * LANES
        parts.append(ref[:, pl.ds(pl.multiple_of(start, LANES), LANES)])
    return jnp.concatenate(parts, axis=1)


def front_kernel(own_ref, peer_ref, cot_ref, peer_cot_ref, momentum_ref, x0_ref, gram_ref):
    rows = x0_ref.shape[0]
    half = own_place()[2]
    cots = jnp.concatenate([cot_ref[...], peer_cot_ref[...]], axis=0)
    gram = None
    block = 2 * LANES
    for i in range(rows // block):
        toks = jnp.concatenate(
            [half_columns(ref, 2 * i, 2, half) for ref in (own_ref, peer_ref)], axis=0
        )
        part = slice(i * block, (i + 1) * block)
        x0 = momentum_rate * momentum_ref[part].astype(f32) + tdot(toks, cots)
        x0 = x0.astype(bf16)
        x0_ref[part] = x0
        middle = x0.shape[1] // 2
        left, right = x0[:, :middle], x0[:, middle:]
        term = (tdot(left, x0), tdot(right, right))
        gram = term if gram is None else (gram[0] + term[0], gram[1] + term[1])
    gram_ref[...] = jnp.concatenate(gram, axis=1).astype(bf16)


def stage_columns(hidden):
    unit = hidden // sum(WIDTHS)
    starts = [unit * sum(WIDTHS[:i]) for i in range(len(WIDTHS))]
    return [slice(start, start + unit * share) for start, share in zip(starts, WIDTHS)]


def renew_pieces(model_width, cols, which, x0_ref, weight_ref, factor, remainder, out_refs):
    group = own_place()[0]
    chunk = out_refs[0].shape[0]
    for k, out_ref in zip(which, out_refs):
        rows = pl.ds(pl.multiple_of((group ^ k) * chunk, chunk), chunk)
        out_ref[...] = renew(
            weight_ref[rows, cols],
            x0_ref[rows, :],
            x0_ref[rows, cols],
            factor,
            remainder,
            model_width,
        )


def update_kernel(
    model_width,
    cols,
    which,
    own_ref,
    peer_ref,
    x0_ref,
    weight_ref,
    remainder_ref,
    factor_ref,
    *refs,
):
    out_refs, scratch = refs[:-7], refs[-7:]
    gram_bf, poly_bf, half_bf, second_bf, poly_ref, half_ref, second_ref = scratch
    hidden = gram_bf.shape[0]
    middle = hidden // 2
    upper = own_ref[...].astype(f32) + peer_ref[...].astype(f32)
    corners = upper[:, :middle] + upper[:, hidden:]
    on_diagonal = lax.broadcasted_iota(jnp.int32, corners.shape, 0) == lax.broadcasted_iota(
        jnp.int32, corners.shape, 1
    )
    norm_sq = jnp.sum(jnp.where(on_diagonal, corners, 0.0), keepdims=True) + gram_eps
    inverse = 1.0 / norm_sq
    lower = jnp.concatenate([upper[:, middle:hidden].T, upper[:, hidden:]], axis=1)
    grams = (upper[:, :hidden], lower)
    blocks = (slice(0, middle), slice(middle, hidden))
    for part, gram in zip(blocks, grams):
        gram_bf[part] = gram.astype(bf16)
    for part, gram in zip(blocks, grams):
        first = gram * inverse
        square = jnp.dot(gram_bf[part], gram_bf[...], preferred_element_type=f32)
        poly = coef_b * first + (coef_c * inverse * inverse) * square
        poly_ref[part] = poly
        poly_bf[part] = poly.astype(bf16)
        half = coef_a * first + inverse * jnp.dot(
            poly_bf[part], gram_bf[...], preferred_element_type=f32
        )
        half_ref[part] = half
        half_bf[part] = half.astype(bf16)
    for part in blocks:
        second = coef_a * half_ref[part] + jnp.dot(
            half_bf[part], poly_bf[...], preferred_element_type=f32
        )
        second_ref[part] = second
        second_bf[part] = second.astype(bf16)
    for part in blocks:
        square = jnp.dot(second_bf[part], second_bf[...], preferred_element_type=f32)
        poly = coef_b * second_ref[part] + coef_c * square
        crossed = jnp.dot(poly.astype(bf16), poly_bf[...], preferred_element_type=f32)
        remainder_ref[part] = (coef_a * (poly_ref[part] + poly) + crossed).astype(bf16)
    factor = lax.rsqrt(norm_sq)
    factor_ref[...] = jnp.broadcast_to(factor, factor_ref.shape)
    remainder = remainder_ref[:, cols]
    renew_pieces(model_width, cols, which, x0_ref, weight_ref, factor, remainder, out_refs)


def later_kernel(model_width, cols, which, remainder_ref, factor_ref, x0_ref, weight_ref, *out_refs):
    remainder = remainder_ref[:, cols]
    factor = factor_ref[:1, :1]
    renew_pieces(model_width, cols, which, x0_ref, weight_ref, factor, remainder, out_refs)


def choose_kernel(
    hosts, old_ref, new_ref, own_ref, peer_ref, ids_ref, peer_ids_ref, which_ref, *out_refs
):
    _, rows, chunk = out_refs[0].shape
    group, plane, half = own_place()
    planes = old_ref.shape[1]
    for k in range(len(out_refs)):
        for rel in range(2):
            wanted_slot = 2 * plane + (half ^ rel)
            owner = lax.div(wanted_slot, hosts)
            expert = new_ref[group ^ k, wanted_slot]
            holder = jnp.int32(0)
            for p in range(planes):
                holder = jnp.where(old_ref[owner, p] == expert, p, holder)
            which_ref[2 * k + rel] = plane ^ holder
    for rel, (ref, ids) in enumerate(((own_ref, ids_ref), (peer_ref, peer_ids_ref))):
        place = lax.broadcasted_iota(jnp.int32, (rows, rows), 0)
        pick = jnp.where(place == ids[...], 1.0, 0.0).astype(bf16)
        for k, out in enumerate(out_refs):
            count = chunk // LANES
            cols = half_columns(ref, (group ^ k) * count, count, half)
            out[rel] = tdot(pick, cols).astype(bf16)


def route_kernel(count, *refs):
    ins, outs, store = refs[:count], refs[count : 2 * count], refs[2 * count]
    group, plane, _ = own_place()
    for k in range(count):
        store[k] = ins[k][...]
    for k in range(count):
        outs[k][...] = store[group ^ plane ^ k]


def project_kernel(count, planes, stages, rel, which_ref, *refs):
    toks, weights = refs[:count], refs[count : count + planes * stages]
    out_ref = refs[count + planes * stages]
    stores = refs[count + planes * stages + 1 :]
    for stage in range(stages):
        for k in range(planes):
            stores[stage][k] = weights[stage * planes + k][...]
    for k in range(count):
        place = which_ref[2 * k + rel]
        start = 0
        for store in stores:
            cols = slice(start, start + store.shape[2])
            start = cols.stop
            got = jnp.dot(toks[k][rel], store[place], preferred_element_type=f32)
            out_ref[k, :, cols] = got.astype(out_ref.dtype)


def join_kernel(count, keep_ref, other_ref, *out_refs):
    for k in range(count):
        out_refs[k][...] = (keep_ref[k] + other_ref[k].astype(f32)).astype(bf16)


def finish_kernel(count, *refs):
    out_ref = refs[-1]
    start = 0
    for tail in range(len(TAILS)):
        mine = refs[tail * count : (tail + 1) * count]
        cols = slice(start, start + mine[0].shape[1])
        start = cols.stop
        out_ref[:, cols] = sum(r[...].astype(f32) for r in mine).astype(out_ref.dtype)


VMEM, SMEM, HBM = pltpu.VMEM, pltpu.SMEM, pltpu.HBM


def call(kernel, arrays, outs, scratch=(), spaces=None, out_spaces=None):
    spaces = spaces or [VMEM] * len(arrays)
    out_spaces = out_spaces or [VMEM] * len(outs)
    made = {
        VMEM: lambda shape, dtype: pltpu.VMEM(shape, dtype),
        SMEM: lambda shape, dtype: pltpu.SMEM(shape, dtype),
        None: jax.ShapeDtypeStruct,
    }
    return pl.pallas_call(
        kernel,
        out_shape=[made[where](*out) for where, out in zip(out_spaces, outs)],
        in_specs=[pl.BlockSpec(memory_space=where or SMEM) for where in spaces],
        out_specs=[pl.BlockSpec(memory_space=where or VMEM) for where in out_spaces],
        scratch_shapes=list(scratch),
        compiler_params=pltpu.CompilerParams(vmem_limit_bytes=16 * 2**20),
    )(
        *[
            a if where is None else pltpu.with_memory_space_constraint(a, where)
            for where, a in zip(spaces, arrays)
        ]
    )


def on_device(tokens, cotangent, weight_halves, momentum_halves, old_map, new_map, row_ids):
    slot_count = lax.axis_size("slot")
    group_count = lax.axis_size("group")
    planes = slot_count // 2
    inputs = (
        tokens,
        cotangent,
        weight_halves[0],
        momentum_halves[0],
        old_map,
        new_map,
        row_ids,
    )
    fits = group_count == planes and planes <= MOST_PERMUTES
    if fits and tokens.shape[1] == 2 * slot_count * LANES:
        return by_permutes(*inputs)
    return by_all_to_all(*inputs)


FIRST = (3, 2, 1)
ACROSS = (3, 2, 1)


def spread(mine, axis, stride, order):
    landed = [mine[0]] + [None] * (len(mine) - 1)
    for k in order:
        if k < len(mine):
            landed[k] = shifted(mine[k], axis, stride, k)
    return landed


def by_permutes(tokens, cotangent, weight, momentum, old_map, new_map, row_ids):
    slot_count = lax.axis_size("slot")
    count = lax.axis_size("group")
    planes = slot_count // 2
    hosts = slot_count // count
    row_count, model_width = tokens.shape
    hidden = cotangent.shape[1]
    half_rows = model_width // 2
    chunk = half_rows // count
    columns = stage_columns(hidden)

    peer_tokens = swapped(tokens)
    peer_cot = swapped(cotangent)

    def loaded(*arrays):
        return call(
            functools.partial(load_kernel, len(arrays)),
            arrays,
            [(a.shape, a.dtype) for a in arrays],
            [pltpu.SemaphoreType.DMA((len(arrays),))],
            spaces=[HBM] * len(arrays),
        )

    tokens_in, cot_in, momentum_in, ids_in = loaded(tokens, cotangent, momentum, row_ids)
    x0, own_gram = call(
        front_kernel,
        [tokens_in, peer_tokens, cot_in, peer_cot, momentum_in],
        [((half_rows, hidden), bf16), ((hidden // 2, hidden + hidden // 2), bf16)],
    )
    peer_gram = swapped(own_gram)
    (weight_in,) = loaded(weight)
    peer_ids = swapped(ids_in)

    which, *token_cuts = call(
        functools.partial(choose_kernel, hosts),
        [old_map, new_map, tokens_in, peer_tokens, ids_in, peer_ids],
        [((2 * count,), jnp.int32)] + [((2, row_count, chunk), bf16)] * count,
        spaces=[None, None] + [VMEM] * 4,
        out_spaces=[SMEM] + [VMEM] * count,
    )

    arrived = []
    for stage, cols in enumerate(columns):
        width = cols.stop - cols.start
        pieces = [None] * count
        behind = [k for k in range(count) if stage or k != FIRST[0]]
        if stage == 0:
            remainder, factor, pieces[FIRST[0]] = call(
                functools.partial(update_kernel, model_width, cols, FIRST[:1]),
                [own_gram, peer_gram, x0, weight_in],
                [((hidden, hidden), bf16), ((8, LANES), f32), ((chunk, width), bf16)],
                [pltpu.VMEM((hidden, hidden), bf16)] * 4
                + [pltpu.VMEM((hidden, hidden), f32)] * 3,
            )
        made = call(
            functools.partial(later_kernel, model_width, cols, behind),
            [remainder, factor, x0, weight_in],
            [((chunk, width), bf16)] * len(behind),
        )
        for k, piece in zip(behind, made):
            pieces[k] = piece
        landed = spread(pieces, "group", 1, FIRST)
        routed = call(
            functools.partial(route_kernel, count),
            landed,
            [((chunk, width), bf16)] * count,
            [pltpu.VMEM((count, chunk, width), bf16)],
        )
        arrived.append(spread(routed, "slot", 2, ACROSS))

    requested = spread(token_cuts, "group", 1, FIRST)

    returned = []
    for stages in TAILS:
        widths = [columns[i].stop - columns[i].start for i in stages]

        def projected(rel, dtype):
            return call(
                functools.partial(project_kernel, count, planes, len(stages), rel),
                [which] + requested + sum((arrived[i] for i in stages), []),
                [((count, row_count, sum(widths)), dtype)],
                [pltpu.VMEM((planes, chunk, width), bf16) for width in widths],
                spaces=[SMEM] + [VMEM] * (count + planes * len(stages)),
            )[0]

        send = projected(1, bf16)
        other = swapped(send)
        keep = projected(0, f32)
        mine = call(
            functools.partial(join_kernel, count),
            [keep, other],
            [((row_count, sum(widths)), bf16)] * count,
        )
        returned += spread(mine, "group", 1, FIRST)
    return call(
        functools.partial(finish_kernel, count),
        returned,
        [((row_count, hidden), bf16)],
        out_spaces=[None],
    )[0]


def by_all_to_all(tokens, cotangent, weight, momentum, old_map, new_map, row_ids):
    slot_count = lax.axis_size("slot")
    group_count = lax.axis_size("group")
    planes = slot_count // 2
    owners = max(1, 2 * group_count // slot_count)
    row_count, model_width = tokens.shape
    hidden = cotangent.shape[1]
    half_rows = model_width // 2
    chunk = half_rows // group_count
    half = lax.axis_index("slot") % 2
    plane = lax.axis_index("slot") // 2
    group = lax.axis_index("group")
    hosts = slot_count // group_count

    from_group = group ^ jnp.arange(group_count)
    wanted_slot = 2 * plane + (half ^ jnp.arange(2))
    experts = new_map[from_group[:, None], wanted_slot[None, :]]
    lists = old_map[wanted_slot // hosts]
    holder = jnp.argmax((lists[None] == experts[:, :, None]).astype(jnp.int32), axis=2)

    peer_cot = swapped(cotangent)
    peer_tokens = swapped(pick_columns(tokens, 1 - half, slot_count))
    own_tokens = pick_columns(tokens, half, slot_count)
    gradient = tdot(own_tokens, cotangent) + tdot(peer_tokens, peer_cot)
    x0 = (momentum_rate * momentum.astype(f32) + gradient).astype(bf16)
    own_gram = tdot(x0, x0).astype(bf16)
    factor, remainder = update_matrix(own_gram.astype(f32) + swapped(own_gram).astype(f32))
    renewed = renew(weight, x0, x0, factor, remainder, model_width)

    pick = (row_ids[0][:, None] == jnp.arange(row_count)[None, :]).astype(bf16)
    chosen = jnp.dot(pick, tokens, preferred_element_type=f32).astype(bf16)
    own_chosen = pick_columns(chosen, half, slot_count)
    peer_chosen = swapped(pick_columns(chosen, 1 - half, slot_count))
    both = jnp.stack([own_chosen, peer_chosen]).reshape(2, row_count, group_count, chunk)
    requested = jnp.stack(exchange(lambda d: both[:, :, d], "group", 1))
    outputs = []
    for cols in (slice(0, hidden // 2), slice(hidden // 2, hidden)):
        width = cols.stop - cols.start
        chunks = renewed[:, cols].reshape(group_count, chunk, width)
        in_plane = jnp.stack(exchange(lambda d: chunks[d], "group", 1))
        by_owner = jnp.take(in_plane, group ^ jnp.arange(group_count), axis=0)
        by_plane = by_owner.reshape(planes, owners, chunk, width)
        arrived = jnp.stack(exchange(lambda d: by_plane[d], "slot", 2))
        partial = [
            jnp.einsum(
                "ktc,kcw->ktw",
                requested[:, rel],
                arrived[plane ^ holder[:, rel], (half ^ rel) * owners // 2],
                preferred_element_type=f32,
            )
            for rel in range(2)
        ]
        other = swapped(partial[1].astype(bf16))
        summed = (partial[0] + other.astype(f32)).astype(bf16)
        by_group = jnp.take(summed, group ^ jnp.arange(group_count), axis=0)
        returned = exchange(lambda d: by_group[d], "group", 1)
        outputs.append(sum(r.astype(f32) for r in returned).astype(bf16))
    return jnp.concatenate(outputs, axis=1)


def solution(mesh):
    placed = (
        P(("group", "slot"), None),
        P(("group", "slot"), None),
        P(("group", "slot"), None, None),
        P(("group", "slot"), None, None),
        P(),
        P(),
        P(("group", "slot"), None),
    )
    return jax.shard_map(
        on_device, mesh=mesh, in_specs=placed, out_specs=P(("group", "slot"), None), check_vma=False
    )
```
